32 devices in a mesh: cand: 2 (over x), expert: 16 (over z, y, core).
Axes of the slice: x: 2, y: 2, z: 4, core: 2. Of those that a mesh axis runs over, the one named last changes fastest.
Arguments:
- tokens: bfloat16 [2048, 2048], P('expert'), may hold values from -6 to 6
- targets: bfloat16 [2048, 2048], P('expert'), may hold values from -3 to 3
- routes: int32 [4096, 2], P(('cand', 'expert')), parts along dimension 0, may hold values from 0 to 3, all different within a row; in each aligned block of 128 rows (0 to 127, 128 to 255, ...) at most 80 rows name the same one
- gate_ints: int32 [4096, 2], P(('cand', 'expert')), parts along dimension 0, may hold values from 1 to 4096
- expert_home: int32 [8], P('cand'), parts along dimension 0, may hold values from 0 to 3, each once
- gate_up: bfloat16 [2, 8192, 2048], P(None, ('cand', 'expert')), parts along dimension 1, may hold values from -0.125 to 0.125
- down_master: float32 [8192, 2048], P(('cand', 'expert')), parts along dimension 0, may hold values from -0.1875 to 0.1875
- moment1: float32 [8192, 2048], P(('cand', 'expert')), parts along dimension 0, may hold values from -3 to 3
- moment2: float32 [8192, 2048], P(('cand', 'expert')), parts along dimension 0, may hold values from 0.005 to 0.05
Outputs:
- step_taken: float32 [8192, 2048], P(('cand', 'expert')), parts along dimension 0
- moment1_new: float32 [8192, 2048], P(('cand', 'expert')), parts along dimension 0
The draws below stay inside these ranges and needn't reach their ends.
There are 2 independent parts, one for each index of `cand`. The reference program is written for one: setup_inputs(seed, part) draws one part's arguments, and reference() takes and returns one part's arrays. A program takes and returns all parts, laid end to end along the dimension named above; an argument that names none is the same for every part. Nothing has to cross between parts.
Inputs may be any that keep to these rules, and one draw needn't show every extreme that they name: `routes`: each row names 2 different experts; among the rows of one device no expert is named more than 80 times, a bound that some block reaches. `expert_home`: a permutation of the experts.
All inputs are finite; a program needn't handle non-finite values.
Results may differ from the reference program's by a relative error of at most 0.007.
Values may be sent and summed in bfloat16 or wider, within the bound.
A program may use at most 128 MiB of HBM per device.

```python
import math
import jax
import jax.numpy as jnp
import numpy as np
from jax import lax

D = 2048
FF_W = 1024
TOP = 2
GROUP = 4
TOK_DEV = 128
TOKENS = 2048
EXPERTS = 4
FF_DEV = 256
HIDDEN_ALL = 4096
CAP = 80
N_EXPERT = 16


def with_ends(result, stream_key, low, largest):
    extent = result.shape
    place = [jax.random.randint(jax.random.fold_in(stream_key, axis), (), 0, extent[axis]) for axis in range(len(extent))]
    result = result.at[tuple(place)].set(low)
    longest = extent.index(max(extent))
    place[longest] = (place[longest] + 1) % extent[longest]
    return result.at[tuple(place)].set(largest)


def shard_levels(rng, shape, cuts, smallest, largest):
    factor_of = 1.0
    for position, shards_of in cuts:
        heights = jax.random.uniform(jax.random.fold_in(jax.random.fold_in(rng, 6), position), (shards_of,), jnp.float32, smallest / len(cuts), largest / len(cuts))
        factor_of = factor_of * jnp.repeat(jnp.exp(heights), shape[position] // shards_of).reshape((-1,) + (1,) * (len(shape) - 1 - position))
    return factor_of


def shared_out(own_key, own, number, rows, amount, top, reach, skew):
    ranking = jax.random.permutation(own_key, amount)
    heavy_load, usual = shares(amount, rows * top, reach, skew, True), shares(amount, rows * top, reach, skew, False)
    places = jnp.arange(amount)

    def named(tallies, rotation):
        used = int((tallies > 0).sum())
        fixed = max(1, used // 4)
        shifted = fixed + (places - fixed + rotation * (used - fixed)) % max(1, amount - fixed)
        return jnp.zeros((amount,), jnp.int32).at[ranking[jnp.where(places < fixed, places, shifted)]].set(jnp.asarray(tallies, jnp.int32))

    tallies = jnp.where(number % 4 == 0, named(heavy_load, number // 4), named(usual, number - number // 4 - 1))
    mixed = jax.random.permutation(jax.random.fold_in(own, 3), amount)
    giver, receiver = mixed[0:amount // 2 * 2:2], mixed[1:amount // 2 * 2:2]
    margin = jnp.minimum(tallies[giver] - 1, reach - tallies[receiver]) // 2
    margin = jnp.where((giver == ranking[0]) | (receiver == ranking[0]) | (tallies[receiver] == 0), 0, jnp.maximum(margin, 0))
    shifted = jax.random.randint(jax.random.fold_in(own, 4), (amount // 2,), 0, 1 << 20) % (margin + 1)
    tallies = tallies.at[giver].add(-shifted).at[receiver].add(shifted)
    members = jnp.searchsorted(jnp.cumsum(tallies), jnp.arange(rows * top), side="right").astype(jnp.int32)
    table = members.reshape(top, rows).T
    table = table[jax.random.permutation(jax.random.fold_in(own, 1), rows)]
    rotation = jax.random.randint(jax.random.fold_in(own, 2), (rows, 1), 0, top)
    return jnp.take_along_axis(table, (jnp.arange(top)[None, :] + rotation) % top, axis=1)


def shares(amount, total, bound, skew, full):
    portions = [(1 << 20) // math.isqrt(standing ** skew) + 1 for standing in range(1, amount + 1)]
    largest = bound if full else min(bound, max(-(-total // amount), total * portions[0] // sum(portions)))
    least = 1 if total - largest >= amount - 1 else 0
    holding, surplus = [largest] + [least] * (amount - 1), total - largest - least * (amount - 1)
    while surplus > 0:
        free = [i for i in range(1, amount) if holding[i] < largest] or [i for i in range(1, amount) if holding[i] < bound]
        mass, left = sum([portions[i] for i in free]), surplus
        for i in free:
            more = min(bound - holding[i], max(1, left * portions[i] // mass), surplus)
            holding[i] = holding[i] + more
            surplus = surplus - more
    return np.array(holding)


def bell_draw(rng, shape, width, most, pieces=(), kind=jnp.bfloat16):
    array = width * jax.random.normal(rng, shape, jnp.float32)
    if pieces:
        array = array * shard_levels(rng, shape, pieces, -0.22, 0.18)
    return jnp.clip(array, -most, most).astype(kind)


def setup_inputs(seed: int = 0, part: int = 0) -> dict:
    key_list = jax.random.split(jax.random.key(seed), 10)
    part_splits = jax.random.split(jax.random.fold_in(key_list[9], part), 10)
    tokens = bell_draw(key_list[0], (TOKENS, D), 1.0, 6.0, ((0, 16),))
    targets = bell_draw(key_list[1], (TOKENS, D), 0.5, 3.0, ((0, 16),))
    routes_keys = jax.random.split(jax.random.fold_in(part_splits[2], 1), TOKENS // TOK_DEV)
    routes_turns = jax.random.permutation(jax.random.fold_in(part_splits[2], 3), TOKENS // TOK_DEV)
    routes = jax.vmap(lambda own, number: shared_out(jax.random.fold_in(part_splits[2], 2), own, number, TOK_DEV, EXPERTS, TOP, CAP, 2))(routes_keys, routes_turns).reshape((TOKENS, TOP))
    gate_ints = with_ends(jax.random.randint(part_splits[3], (TOKENS, TOP), 1, 4097), jax.random.fold_in(part_splits[3], 1), 1, 4096).astype(jnp.int32)
    expert_home = jax.random.permutation(part_splits[4], EXPERTS).astype(jnp.int32)
    gate_up = bell_draw(part_splits[5], (2, HIDDEN_ALL, D), D ** -0.5, 0.125, ((1, 16),))
    down_master = bell_draw(part_splits[6], (HIDDEN_ALL, D), FF_W ** -0.5, 0.1875, ((0, 16),), jnp.float32)
    moment1 = bell_draw(part_splits[7], (HIDDEN_ALL, D), 0.5, 3.0, ((0, 16),), jnp.float32)
    moment2 = jnp.clip(jnp.exp(math.log(0.05) - 2.3025851 * jax.random.uniform(part_splits[8], (HIDDEN_ALL, D), jnp.float32) ** shard_levels(part_splits[8], (HIDDEN_ALL, D), ((0, 16),), -0.2, 0.2)), 0.005, 0.05)
    return dict(tokens=tokens, targets=targets, routes=routes, gate_ints=gate_ints, expert_home=expert_home, gate_up=gate_up, down_master=down_master, moment1=moment1, moment2=moment2)


learn_rate = 0.02
epsilon = 1e-08
prior_steps = 20
loss_scale = 0.125

def adam_step(master, moment_one, moment_two, gradient, count):
    moment_one = 0.9 * moment_one + 0.1 * gradient
    moment_two = 0.999 * moment_two + 0.001 * gradient * gradient
    first_fix = 1.0 - 0.9 ** (prior_steps + count)
    second_fix = 1.0 - 0.999 ** (prior_steps + count)
    master = master - learn_rate * (moment_one / first_fix) / (jnp.sqrt(moment_two / second_fix) + epsilon)
    return (master, moment_one, moment_two)

def reference(tokens, targets, routes, gate_ints, expert_home, gate_up, down_master, moment1, moment2):
    slot_count = N_EXPERT * CAP
    flat_ids = routes.reshape(N_EXPERT, TOK_DEV * TOP)
    onehot = (flat_ids[:, :, None] == jnp.arange(EXPERTS, dtype=jnp.int32)[None, None, :]).astype(jnp.int32)
    slot_rank = lax.optimization_barrier(jnp.sum((jnp.cumsum(onehot, axis=1) - onehot) * onehot, axis=2))
    sources = jnp.arange(N_EXPERT, dtype=jnp.int32)[:, None]
    slot_dest = (flat_ids * slot_count + sources * CAP + slot_rank).reshape(-1).astype(jnp.int32)
    token_index = jnp.repeat(jnp.arange(TOKENS, dtype=jnp.int32), TOP)
    weights = gate_ints.reshape(-1).astype(jnp.float32) / 4096.0
    buffer = jnp.zeros((EXPERTS * slot_count, D), jnp.bfloat16).at[slot_dest].set(tokens[token_index])
    buffer = buffer.reshape(EXPERTS, slot_count, D)
    expert_ids = jnp.arange(EXPERTS, dtype=jnp.int32)

    def expert_hidden(inputs):
        expert, arrived = inputs
        row_start = (expert_home[expert] * FF_W).astype(jnp.int32)
        gate_rows = lax.dynamic_slice_in_dim(gate_up[0], row_start, FF_W, 0)
        up_rows = lax.dynamic_slice_in_dim(gate_up[1], row_start, FF_W, 0)
        gate_acts = lax.dot_general(arrived, gate_rows, (((1,), (1,)), ((), ())), preferred_element_type=jnp.float32)
        up_acts = lax.dot_general(arrived, up_rows, (((1,), (1,)), ((), ())), preferred_element_type=jnp.float32)
        return (jax.nn.silu(gate_acts) * up_acts).astype(jnp.bfloat16)
    hiddens = lax.map(expert_hidden, (expert_ids, buffer))

    def expert_output(inputs, master_low):
        expert, hidden = inputs
        row_start = (expert_home[expert] * FF_W).astype(jnp.int32)
        down_rows = lax.dynamic_slice_in_dim(master_low, row_start, FF_W, 0)
        summed = jnp.zeros((slot_count, D), jnp.float32)
        for member in range(GROUP):
            lower_edge = member * FF_DEV
            partial_value = jnp.dot(hidden[:, lower_edge:lower_edge + FF_DEV], down_rows[lower_edge:lower_edge + FF_DEV], preferred_element_type=jnp.float32).astype(jnp.bfloat16)
            summed = summed + partial_value.astype(jnp.float32)
        return summed

    def expert_grad(inputs):
        hidden, grad_rows = inputs
        return lax.dot_general(hidden, grad_rows, (((0,), (0,)), ((), ())), preferred_element_type=jnp.float32)
    master, moment_one, moment_two = (down_master, moment1, moment2)
    for round_index in range(2):
        master_low = master.astype(jnp.bfloat16)
        outputs = lax.map(lambda inputs: expert_output(inputs, master_low), (expert_ids, hiddens))
        picked = outputs.reshape(EXPERTS * slot_count, D)[slot_dest] * weights[:, None]
        mixed = lax.optimization_barrier(jnp.sum(picked.reshape(TOKENS, TOP, D), axis=1))
        residual = (mixed - targets.astype(jnp.float32)) * loss_scale
        grad_slots = (weights[:, None] * residual[token_index]).astype(jnp.bfloat16)
        grad_buffer = jnp.zeros((EXPERTS * slot_count, D), jnp.bfloat16).at[slot_dest].set(grad_slots)
        grads = lax.map(expert_grad, (hiddens, grad_buffer.reshape(EXPERTS, slot_count, D)))
        gradient = jnp.zeros((EXPERTS, FF_W, D), jnp.float32).at[expert_home].set(grads).reshape(HIDDEN_ALL, D)
        master, moment_one, moment_two = adam_step(master, moment_one, moment_two, gradient, round_index + 1)
    return ((down_master - master) / learn_rate, moment_one)
```

```python
import functools

import jax
import jax.numpy as jnp
from jax import lax
from jax.experimental import pallas as pl
from jax.experimental.pallas import tpu as pltpu
from jax.sharding import PartitionSpec as P

GROUP = 4
CHUNKS = 2

learn_rate = 0.02
epsilon = 1e-08
prior_steps = 20
loss_scale = 0.125


def xor(index, mask, bits):
    result = index
    for bit in range(bits):
        if mask >> bit & 1:
            result = result + (1 << bit) * (1 - 2 * lax.rem(index // (1 << bit), 2))
    return result


def push(source, target, send_sem, recv_sem, peer):
    return pltpu.make_async_remote_copy(
        src_ref=source,
        dst_ref=target,
        send_sem=send_sem,
        recv_sem=recv_sem,
        device_id={"expert": peer},
        device_id_type=pl.DeviceIdType.MESH,
    )


def refit_kernel(
    groups, capacity,
    home, routes, gates, tokens, targets, gate_up, master, first, second,
    moved_out, first_out,
    outgoing, arrived, weights_in, hidden, loaded, low, master_in, first_in, second_in, goal,
    plan, picks, picks_t, scales, sum_out, sum_in, grad_out, grad_in, values,
    master_two, first_two, second_two, moved_one, moved_rows, first_rows,
    load_sems, plan_send, plan_recv, group_send, group_recv, row_send, row_recv,
    unit_send, unit_recv, state_send, state_recv, send_sems, recv_sems, out_send, out_recv,
):
    bf16, f32 = jnp.bfloat16, jnp.float32
    here = lax.axis_index("expert")
    me, member = here // GROUP, lax.rem(here, GROUP)
    base = me * GROUP
    bits = groups.bit_length() - 1
    top_count, tok = routes.shape
    feat = tokens.shape[1]
    units = master.shape[0]
    width = feat // GROUP
    part = width // CHUNKS
    block = GROUP * capacity
    span_all = groups * capacity
    order = list(range(1, groups))
    chain = [0] + order
    masks = range(1, GROUP)

    def group_of(d):
        return xor(me, d, bits)

    def partner(mask):
        return base + xor(member, mask, 2)

    def across(d):
        return group_of(d) * GROUP + member

    loads = [
        pltpu.make_async_copy(source, target, load_sems.at[i])
        for i, (source, target) in enumerate((
            (gate_up, weights_in), (master, loaded.at[0]), (first, loaded.at[1]),
            (second, loaded.at[2]),
        ))
    ]
    for copy in (loads[1], loads[0], loads[2], loads[3]):
        copy.start()

    barrier = pltpu.get_barrier_semaphore()
    peers = [across(d) for d in order] + [partner(mask) for mask in masks]
    for peer in peers:
        pl.semaphore_signal(
            barrier, inc=1, device_id={"expert": peer}, device_id_type=pl.DeviceIdType.MESH
        )

    sub = lax.broadcasted_iota(jnp.int32, (tok, tok), 0)
    lane = lax.broadcasted_iota(jnp.int32, (tok, tok), 1)
    on_diagonal = sub == lane

    def upright(row):
        return jnp.sum(jnp.where(on_diagonal, row, 0.0), axis=1, keepdims=True)

    chosen = [routes[pl.ds(k, 1), :] for k in range(top_count)]
    chosen_f = [c.astype(f32) for c in chosen]
    standing = [upright(c) for c in chosen_f]
    for k in range(top_count):
        same = jnp.zeros((tok, tok), f32)
        for other in range(top_count):
            same = same + jnp.where(standing[other] == chosen_f[k], 1.0, 0.0)
        rank = jnp.sum(jnp.where(sub < lane, same, 0.0), axis=0, keepdims=True)
        place = jnp.zeros((1, tok), jnp.int32)
        for expert in range(home.shape[0]):
            place = place + jnp.where(chosen[k] == expert, home[expert], 0)
        plan[0, pl.ds(k, 1), :] = place.astype(f32) * capacity + rank
        plan[0, pl.ds(top_count + k, 1), :] = gates[pl.ds(k, 1), :].astype(f32) / 4096.0

    def own_rows(d):
        rows = lax.broadcasted_iota(jnp.int32, (capacity, tok), 0) + group_of(d) * capacity
        rows = rows.astype(f32)
        pick = jnp.zeros((capacity, tok), f32)
        for k in range(top_count):
            pick = jnp.where(plan[0, pl.ds(k, 1), :] == rows, 1.0, pick)
        return jnp.dot(pick.astype(bf16), tokens[...], preferred_element_type=f32).astype(bf16)

    def plan_copy(mask):
        return push(
            plan.at[0], plan.at[mask], plan_send.at[mask - 1], plan_recv.at[mask - 1],
            partner(mask),
        )

    def group_copy(d):
        return push(
            outgoing.at[d], arrived.at[d, 0], group_send.at[d], group_recv.at[d], across(d)
        )

    def row_copy(d, mask):
        source = arrived.at[d, 2 if mask == 3 else 0]
        return push(
            source, arrived.at[d, mask], row_send.at[d, mask - 1], row_recv.at[d, mask - 1],
            partner(1 if mask == 3 else mask),
        )

    def unit_copy(d, mask, index):
        flip = 1 if mask == 3 else mask
        origin = 2 if mask == 3 else 0
        return push(
            hidden.at[d, index, :, pl.ds(origin * units, units)],
            hidden.at[d, index ^ flip, :, pl.ds(mask * units, units)],
            unit_send.at[d, mask - 1, index], unit_recv.at[d, mask - 1, index], partner(flip),
        )

    states = (
        (low.at[0], master_in), (targets, goal), (low.at[1], first_in), (low.at[2], second_in)
    )

    def state_copy(which, mask):
        source, target = states[which]
        rows = source.shape[0]
        column = pl.multiple_of(xor(member, mask, 2) * width, 128)
        return push(
            source.at[:, pl.ds(column, width)], target.at[pl.ds(mask * rows, rows)],
            state_send.at[which, mask - 1], state_recv.at[which, mask - 1], partner(mask),
        )

    def own_slice(which):
        source, target = states[which]
        column = pl.multiple_of(member * width, 128)
        target[pl.ds(0, source.shape[0])] = source[:, pl.ds(column, width)]

    def travel(source, target, phase, chunk, d):
        return push(
            source.at[phase // 2, chunk, d], target.at[phase // 2, chunk, d],
            send_sems.at[phase, chunk, d], recv_sems.at[phase, chunk, d], across(d),
        )

    def columns(chunk):
        return pl.ds(chunk * part, part)

    def lower(which):
        loads[which + 1].wait()

        @pl.loop(0, units // 16)
        def _(tile):
            span = pl.ds(pl.multiple_of(tile * 16, 16), 16)
            low[which, span] = loaded[which, span].astype(bf16)

    pl.semaphore_wait(barrier, len(peers))
    for d in order:
        outgoing[d] = own_rows(d)
        group_copy(d).start()
    arrived[0, 0] = own_rows(0)
    row_copy(0, 2).start()
    row_copy(0, 1).start()
    for mask in masks:
        plan_copy(mask).start()
    lower(0)
    row_copy(0, 2).wait_recv()
    row_copy(0, 3).start()
    for mask in (2, 3, 1):
        state_copy(0, mask).start()
    own_slice(0)
    for mask in masks:
        plan_copy(mask).wait_recv()

    for index in range(GROUP):
        for k in range(top_count):
            scales[k, index] = upright(plan[index, pl.ds(top_count + k, 1), :])
            slot = upright(plan[index, pl.ds(k, 1), :])
            for d in chain:
                rows = lax.broadcasted_iota(jnp.int32, (tok, capacity), 1)
                rows = (rows + group_of(d) * capacity).astype(f32)
                picks[k, index, :, pl.ds(d * capacity, capacity)] = jnp.where(
                    slot == rows, 1.0, 0.0
                ).astype(bf16)
        for d in chain:
            rows = lax.broadcasted_iota(jnp.int32, (capacity, tok), 0)
            rows = (rows + group_of(d) * capacity).astype(f32)
            for k in range(top_count):
                picks_t[index, pl.ds(d * capacity, capacity), pl.ds(k * tok, tok)] = jnp.where(
                    plan[index, pl.ds(k, 1), :] == rows, 1.0, 0.0
                ).astype(bf16)

    def compute(d):
        row_copy(d, 1).wait_recv()
        row_copy(d, 3).wait_recv()
        acts = [
            lax.dot_general(
                arrived[d].reshape(block, feat), weights_in[i], (((1,), (1,)), ((), ())),
                preferred_element_type=f32,
            )
            for i in range(2)
        ]
        gated = acts[0] / (1.0 + jnp.exp(-acts[0])) * acts[1]
        hidden[d, :, :, pl.ds(0, units)] = gated.astype(bf16).reshape(GROUP, capacity, units)
        for mask in (2, 1):
            for index in range(GROUP):
                unit_copy(d, mask, index).start()

    def pass_units(d):
        for index in range(GROUP):
            unit_copy(d, 2, index).wait_recv()
        for index in range(GROUP):
            unit_copy(d, 3, index).start()

    def units_here(d):
        for index in range(GROUP):
            unit_copy(d, 1, index).wait_recv()
            unit_copy(d, 3, index).wait_recv()

    def forward(step, chunk, d):
        weight = master_in if step == 0 else master_two
        result = jnp.dot(
            hidden[d].reshape(block, GROUP * units), weight[:, columns(chunk)],
            preferred_element_type=f32,
        ).astype(bf16).reshape(GROUP, capacity, part)
        if d:
            sum_out[step, chunk, d] = result
            travel(sum_out, sum_in, 2 * step, chunk, d).start()
        else:
            sum_in[step, chunk, d] = result

    loads[0].wait()
    for position, d in enumerate(order):
        group_copy(d).wait_recv()
        row_copy(d, 2).start()
        row_copy(d, 1).start()
        compute(chain[position])
        row_copy(d, 2).wait_recv()
        row_copy(d, 3).start()
        if position:
            pass_units(chain[position - 1])
        if position == 1:
            for mask in masks:
                state_copy(0, mask).wait_recv()
        if position > 1:
            units_here(chain[position - 1])
            for chunk in range(CHUNKS):
                forward(0, chunk, chain[position - 1])
    compute(chain[-1])
    for d in chain[-2:]:
        pass_units(d)
    for which in (1, 2, 3):
        if which > 1:
            lower(which - 1)
        for mask in (2, 3, 1):
            state_copy(which, mask).start()
        own_slice(which)
    units_here(chain[-2])
    for chunk in range(CHUNKS):
        forward(0, chunk, chain[-2])
    units_here(chain[-1])
    for chunk in range(CHUNKS):
        forward(0, chunk, chain[-1])
    units_here(0)
    for chunk in range(CHUNKS):
        forward(0, chunk, 0)
    for mask in masks:
        state_copy(1, mask).wait_recv()

    def arrive(source, target, phase, chunk):
        for d in order:
            travel(source, target, phase, chunk, d).wait_recv()

    def residuals(step, chunk):
        arrive(sum_out, sum_in, 2 * step, chunk)
        for index in range(GROUP):
            mixed = jnp.zeros((tok, part), f32)
            for k in range(top_count):
                mixed = mixed + scales[k, index] * jnp.dot(
                    picks[k, index], sum_in[step, chunk, :, index].reshape(span_all, part),
                    preferred_element_type=f32,
                )
            aim = goal[pl.ds(index * tok, tok), columns(chunk)].astype(f32)
            residual = (mixed - aim) * loss_scale
            for k in range(top_count):
                values[pl.ds(k * tok, tok)] = (scales[k, index] * residual).astype(bf16)
            rows = jnp.dot(
                picks_t[index], values[...], preferred_element_type=f32
            ).astype(bf16).reshape(groups, capacity, part)
            for d in order:
                grad_out[step, chunk, d, index] = rows[d]
            grad_in[step, chunk, 0, index] = rows[0]
        for d in order:
            travel(grad_out, grad_in, 2 * step + 1, chunk, d).start()

    results = ((moved_rows, moved_out), (first_rows, first_out))

    def out_columns(chunk):
        return pl.ds(pl.multiple_of(member * width + chunk * part, 128), part)

    def out_copy(which, chunk, mask):
        source, target = results[which]
        return push(
            source.at[pl.ds(mask * units, units), columns(chunk)],
            target.at[:, out_columns(chunk)],
            out_send.at[which, chunk, mask - 1], out_recv.at[which, chunk, mask - 1],
            partner(mask),
        )

    def update(step, chunk):
        arrive(grad_out, grad_in, 2 * step + 1, chunk)
        count = step + 1
        first_fix = 1.0 - 0.9 ** (prior_steps + count)
        second_fix = 1.0 - 0.999 ** (prior_steps + count)
        cols = columns(chunk)
        for mask in (2, 3, 1, 0):
            span = pl.ds(mask * units, units)
            gradient = lax.dot_general(
                hidden[:, :, :, span].reshape(groups * block, units),
                grad_in[step, chunk].reshape(groups * block, part),
                (((0,), (0,)), ((), ())), preferred_element_type=f32,
            )
            one = (first_in if step == 0 else first_two)[span, cols].astype(f32)
            two = (second_in if step == 0 else second_two)[span, cols].astype(f32)
            one = 0.9 * one + 0.1 * gradient
            two = 0.999 * two + 0.001 * gradient * gradient
            change = (one / first_fix) / (jnp.sqrt(two / second_fix) + epsilon)
            if step == 0:
                first_two[span, cols] = one
                second_two[span, cols] = two
                moved_one[span, cols] = change
                old = master_in[span, cols].astype(f32)
                master_two[span, cols] = (old - learn_rate * change).astype(bf16)
            else:
                moved = (moved_one[span, cols] + change).astype(bf16)
                if mask:
                    moved_rows[span, cols] = moved
                    first_rows[span, cols] = one.astype(bf16)
                    for which in range(2):
                        out_copy(which, chunk, mask).start()
                else:
                    moved_out[:, out_columns(chunk)] = moved
                    first_out[:, out_columns(chunk)] = one.astype(bf16)

    for step in range(2):
        for chunk in range(CHUNKS):
            residuals(step, chunk)
        if step == 0:
            for which in (2, 3):
                for mask in masks:
                    state_copy(which, mask).wait_recv()
        for chunk in range(CHUNKS):
            update(step, chunk)
            if step == 0:
                for d in order + [0]:
                    forward(1, chunk, d)

    for mask in masks:
        plan_copy(mask).wait_send()
        for which in range(4):
            state_copy(which, mask).wait_send()
        for d in chain:
            row_copy(d, mask).wait_send()
            for index in range(GROUP):
                unit_copy(d, mask, index).wait_send()
    for d in order:
        group_copy(d).wait_send()
        for phase in range(4):
            source, target = ((sum_out, sum_in), (grad_out, grad_in))[phase % 2]
            for chunk in range(CHUNKS):
                travel(source, target, phase, chunk, d).wait_send()
    for chunk in range(CHUNKS):
        for which in range(2):
            for mask in masks:
                out_copy(which, chunk, mask).wait()


def refit(groups, capacity, home, routes, gates, tokens, targets, gate_up, master, first, second):
    bf16, f32 = jnp.bfloat16, jnp.float32
    top_count, tok = routes.shape
    units, feat = master.shape
    width = feat // GROUP
    slots = groups * capacity
    vmem = pl.BlockSpec(memory_space=pltpu.VMEM)
    hbm = pl.BlockSpec(memory_space=pl.ANY)
    buffer = lambda *shape, kind=bf16: pltpu.VMEM(shape, kind)
    pair = lambda *shape: [pltpu.SemaphoreType.DMA(shape)] * 2
    exchange = buffer(2, CHUNKS, groups, GROUP, capacity, width // CHUNKS)
    return pl.pallas_call(
        functools.partial(refit_kernel, groups, capacity),
        out_shape=[jax.ShapeDtypeStruct((units, feat), bf16)] * 2,
        in_specs=[pl.BlockSpec(memory_space=pltpu.SMEM)] + [vmem] * 4 + [hbm] * 4,
        out_specs=[vmem] * 2,
        scratch_shapes=[
            buffer(groups, capacity, feat),
            buffer(groups, GROUP, capacity, feat),
            buffer(*gate_up.shape),
            buffer(groups, GROUP, capacity, GROUP * units),
            buffer(3, units, feat, kind=f32),
            buffer(3, units, feat),
            *[buffer(GROUP * units, width)] * 3,
            buffer(GROUP * tok, width),
            buffer(GROUP, max(8, 2 * top_count), tok, kind=f32),
            buffer(top_count, GROUP, tok, slots),
            buffer(GROUP, slots, top_count * tok),
            buffer(top_count, GROUP, tok, 1, kind=f32),
            *[exchange] * 4,
            buffer(top_count * tok, width // CHUNKS),
            buffer(GROUP * units, width),
            *[buffer(GROUP * units, width, kind=f32)] * 3,
            *[buffer(GROUP * units, width)] * 2,
            pltpu.SemaphoreType.DMA((4,)),
            *pair(3), *pair(groups), *pair(groups, 3), *pair(groups, 3, GROUP), *pair(4, 3),
            *pair(4, CHUNKS, groups), *pair(2, CHUNKS, 3),
        ],
        compiler_params=pltpu.CompilerParams(
            collective_id=0, has_side_effects=True, vmem_limit_bytes=62 * 2**20
        ),
    )(home, routes, gates, tokens, targets, gate_up, master, first, second)


def shards(tokens, targets, routes, gate_ints, expert_home, gate_up, down_master, moment1, moment2):
    devices = lax.axis_size("expert")
    tok_rows, top_count = routes.shape
    groups = devices // GROUP
    capacity = (5 * tok_rows * top_count * GROUP + 4 * devices - 1) // (4 * devices)
    capacity = -(-capacity // 16) * 16
    moved, moment_one = refit(
        groups, capacity, expert_home, routes.T, gate_ints.T, tokens, targets, gate_up,
        down_master, moment1, moment2,
    )
    return moved.astype(jnp.float32), moment_one.astype(jnp.float32)


def solution(mesh):
    in_specs = (
        P("expert", None),
        P("expert", None),
        P(("cand", "expert"), None),
        P(("cand", "expert"), None),
        P("cand"),
        P(None, ("cand", "expert"), None),
        P(("cand", "expert"), None),
        P(("cand", "expert"), None),
        P(("cand", "expert"), None),
    )
    out_specs = (P(("cand", "expert"), None), P(("cand", "expert"), None))
    return jax.shard_map(shards, mesh=mesh, in_specs=in_specs, out_specs=out_specs, check_vma=False)
```

```python
import functools

import jax
import jax.numpy as jnp
from jax import lax
from jax.experimental import pallas as pl
from jax.experimental.pallas import tpu as pltpu
from jax.sharding import PartitionSpec as P

GROUP = 4
CHUNKS = 4

learn_rate = 0.02
epsilon = 1e-08
prior_steps = 20
loss_scale = 0.125


def xor(index, mask, bits):
    result = index
    for bit in range(bits):
        if mask >> bit & 1:
            result = result + (1 << bit) * (1 - 2 * lax.rem(index // (1 << bit), 2))
    return result


def push(source, target, send_sem, recv_sem, peer):
    return pltpu.make_async_remote_copy(
        src_ref=source,
        dst_ref=target,
        send_sem=send_sem,
        recv_sem=recv_sem,
        device_id={"expert": peer},
        device_id_type=pl.DeviceIdType.MESH,
    )


def refit_kernel(
    groups, capacity,
    home, routes, gates, tokens, targets, gate_up, master, first, second,
    moved_out, first_out,
    outgoing, arrived, weights_in, hidden, loaded, low, master_in, first_in, second_in, goal,
    plan, picks, picks_t, scales, sums_all, sums, near_out, dense_out, dense_in, even_out, even_in,
    grad_out, grad_in, values,
    master_two, first_two, second_two, moved_one, moved_rows, first_rows,
    load_sems, plan_send, plan_recv, far_send, far_recv, group_send, group_recv, row_send, row_recv,
    unit_send, unit_recv, state_send, state_recv, send_sems, recv_sems,
    dense_send, dense_recv, out_send, out_recv,
):
    bf16, f32 = jnp.bfloat16, jnp.float32
    here = lax.axis_index("expert")
    me, member = here // GROUP, lax.rem(here, GROUP)
    base = me * GROUP
    bits = groups.bit_length() - 1
    top_count, tok = routes.shape
    feat = tokens.shape[1]
    units = master.shape[0]
    width = feat // GROUP
    part = width // CHUNKS
    block = GROUP * capacity
    line = groups == 4
    sides = (0, 2, 3) if line else (0,)
    reach = 2 if line else groups
    span_all = reach * capacity
    inner = (me + 1) // 2 == 1
    order = list(range(2, groups)) + [1]
    chain = [0] + order
    masks = range(1, GROUP)

    def group_of(d):
        return xor(me, d, bits)

    def partner(mask):
        return base + xor(member, mask, 2)

    def across(d):
        return group_of(d) * GROUP + member

    loads = [
        pltpu.make_async_copy(source, target, load_sems.at[i])
        for i, (source, target) in enumerate((
            (gate_up, weights_in), (master, loaded.at[0]), (first, loaded.at[1]),
            (second, loaded.at[2]),
        ))
    ]
    for copy in (loads[1], loads[0], loads[2], loads[3]):
        copy.start()

    barrier = pltpu.get_barrier_semaphore()
    peers = [across(d) for d in order] + [partner(mask) for mask in masks]
    for peer in peers:
        pl.semaphore_signal(
            barrier, inc=1, device_id={"expert": peer}, device_id_type=pl.DeviceIdType.MESH
        )

    sub = lax.broadcasted_iota(jnp.int32, (tok, tok), 0)
    lane = lax.broadcasted_iota(jnp.int32, (tok, tok), 1)
    on_diagonal = sub == lane

    def upright(row):
        return jnp.sum(jnp.where(on_diagonal, row, 0.0), axis=1, keepdims=True)

    chosen = [routes[pl.ds(k, 1), :] for k in range(top_count)]
    chosen_f = [c.astype(f32) for c in chosen]
    standing = [upright(c) for c in chosen_f]
    for k in range(top_count):
        same = jnp.zeros((tok, tok), f32)
        for other in range(top_count):
            same = same + jnp.where(standing[other] == chosen_f[k], 1.0, 0.0)
        rank = jnp.sum(jnp.where(sub < lane, same, 0.0), axis=0, keepdims=True)
        place = jnp.zeros((1, tok), jnp.int32)
        for expert in range(home.shape[0]):
            place = place + jnp.where(chosen[k] == expert, home[expert], 0)
        plan[0, 0, pl.ds(k, 1), :] = place.astype(f32) * capacity + rank
        plan[0, 0, pl.ds(top_count + k, 1), :] = gates[pl.ds(k, 1), :].astype(f32) / 4096.0

    def own_rows(d):
        rows = lax.broadcasted_iota(jnp.int32, (capacity, tok), 0) + group_of(d) * capacity
        rows = rows.astype(f32)
        pick = jnp.zeros((capacity, tok), f32)
        for k in range(top_count):
            pick = jnp.where(plan[0, 0, pl.ds(k, 1), :] == rows, 1.0, pick)
        return jnp.dot(pick.astype(bf16), tokens[...], preferred_element_type=f32).astype(bf16)

    def plan_copy(mask):
        return push(
            plan.at[0, 0], plan.at[0, mask], plan_send.at[mask - 1], plan_recv.at[mask - 1],
            partner(mask),
        )

    def group_copy(d):
        return push(
            outgoing.at[d], arrived.at[d, 0], group_send.at[d], group_recv.at[d], across(d)
        )

    def row_copy(d, mask):
        source = arrived.at[d, 2 if mask == 3 else 0]
        return push(
            source, arrived.at[d, mask], row_send.at[d, mask - 1], row_recv.at[d, mask - 1],
            partner(1 if mask == 3 else mask),
        )

    def unit_copy(d, mask, index):
        flip = 1 if mask == 3 else mask
        origin = 2 if mask == 3 else 0
        return push(
            hidden.at[d, index, :, pl.ds(origin * units, units)],
            hidden.at[d, index ^ flip, :, pl.ds(mask * units, units)],
            unit_send.at[d, mask - 1, index], unit_recv.at[d, mask - 1, index], partner(flip),
        )

    states = (
        (low.at[0], master_in), (targets, goal), (low.at[1], first_in), (low.at[2], second_in)
    )

    def state_copy(which, mask):
        source, target = states[which]
        rows = source.shape[0]
        column = pl.multiple_of(xor(member, mask, 2) * width, 128)
        return push(
            source.at[:, pl.ds(column, width)], target.at[pl.ds(mask * rows, rows)],
            state_send.at[which, mask - 1], state_recv.at[which, mask - 1], partner(mask),
        )

    def own_slice(which):
        source, target = states[which]
        column = pl.multiple_of(member * width, 128)
        target[pl.ds(0, source.shape[0])] = source[:, pl.ds(column, width)]

    def far_plan(d):
        return push(plan.at[0], plan.at[d - 1], far_send, far_recv.at[d - 1], across(d))

    def travel(source, target, phase, chunk, d, to):
        return push(
            source, target, send_sems.at[phase, chunk, to], recv_sems.at[phase, chunk, to],
            across(d),
        )

    def sums_copy(step, chunk, d):
        if not (line and step):
            return travel(
                near_out.at[step, chunk, d], sums_all.at[step, chunk, :, d], 2 * step, chunk, d, d
            )
        to = sides.index(d ^ 1)
        source = near_out.at[step, chunk, 0] if d == 1 else sums.at[chunk, d - 1, :, 0]
        return travel(source, sums.at[chunk, to, :, 1], 2 * step, chunk, 1, to)

    def grads_copy(step, chunk, q, d):
        source = grad_out.at[step, chunk, sides.index(q) if line else d]
        to = q ^ 1 if line else d
        return travel(source, grad_in.at[step, chunk, to], 2 * step + 1, chunk, d, to)

    def dense_copy(step, chunk, q):
        return push(
            dense_out.at[step, chunk, q - 2], dense_in.at[step, chunk],
            dense_send.at[step, chunk, q - 2], dense_recv.at[step, chunk, 2], across(q),
        )

    def even_copy(step, chunk, q):
        return push(
            even_out.at[step, chunk], even_in.at[step, chunk, q - 2],
            dense_send.at[step, chunk, 2], dense_recv.at[step, chunk, q - 2], across(q),
        )

    def columns(chunk):
        return pl.ds(chunk * part, part)

    def lower(which):
        loads[which + 1].wait()

        @pl.loop(0, units // 16)
        def _(tile):
            span = pl.ds(pl.multiple_of(tile * 16, 16), 16)
            low[which, span] = loaded[which, span].astype(bf16)

    pl.semaphore_wait(barrier, len(peers))
    early = order[: groups // 4]
    arrived[0, 0] = own_rows(0)
    row_copy(0, 2).start()
    row_copy(0, 1).start()
    for d in order:
        outgoing[d] = own_rows(d)
        if d in early:
            group_copy(d).start()
    for mask in masks:
        plan_copy(mask).start()
    lower(0)
    row_copy(0, 2).wait_recv()
    row_copy(0, 3).start()
    for d in order:
        if d not in early:
            group_copy(d).start()
    for mask in (2, 3, 1):
        state_copy(0, mask).start()
    own_slice(0)
    for mask in masks:
        plan_copy(mask).wait_recv()

    def make_picks(side):
        for index in range(GROUP):
            for k in range(top_count):
                scales[side, k, index] = upright(plan[side, index, pl.ds(top_count + k, 1), :])
                slot = upright(plan[side, index, pl.ds(k, 1), :])
                for d in range(reach if side else groups):
                    rows = lax.broadcasted_iota(jnp.int32, (tok, capacity), 1)
                    rows = (rows + group_of(d) * capacity).astype(f32)
                    picks[side, k, index, :, pl.ds(d * capacity, capacity)] = jnp.where(
                        slot == rows, 1.0, 0.0
                    ).astype(bf16)
            for d in range(reach):
                rows = lax.broadcasted_iota(jnp.int32, (capacity, tok), 0)
                rows = (rows + group_of(d) * capacity).astype(f32)
                for k in range(top_count):
                    picks_t[
                        side, index, pl.ds(d * capacity, capacity), pl.ds(k * tok, tok)
                    ] = jnp.where(
                        plan[side, index, pl.ds(k, 1), :] == rows, 1.0, 0.0
                    ).astype(bf16)

    if line:

        @pl.when(inner)
        def _():
            far_plan(3).start()

        @pl.when(jnp.logical_not(inner))
        def _():
            far_plan(2).start()

    make_picks(0)

    def compute(d):
        row_copy(d, 1).wait_recv()
        row_copy(d, 3).wait_recv()
        acts = [
            lax.dot_general(
                arrived[d].reshape(block, feat), weights_in[i], (((1,), (1,)), ((), ())),
                preferred_element_type=f32,
            )
            for i in range(2)
        ]
        gated = acts[0] / (1.0 + jnp.exp(-acts[0])) * acts[1]
        hidden[d, :, :, pl.ds(0, units)] = gated.astype(bf16).reshape(GROUP, capacity, units)
        for mask in (2, 1):
            for index in range(GROUP):
                unit_copy(d, mask, index).start()

    def pass_units(d):
        for index in range(GROUP):
            unit_copy(d, 2, index).wait_recv()
        for index in range(GROUP):
            unit_copy(d, 3, index).start()

    def units_here(d):
        for index in range(GROUP):
            unit_copy(d, 1, index).wait_recv()
            unit_copy(d, 3, index).wait_recv()

    def forward(step, chunk, d):
        weight = master_in if step == 0 else master_two
        result = jnp.dot(
            hidden[d].reshape(block, GROUP * units), weight[:, columns(chunk)],
            preferred_element_type=f32,
        ).astype(bf16).reshape(GROUP, capacity, part)
        if not (line and step):
            if d:
                near_out[step, chunk, d] = result
                sums_copy(step, chunk, d).start()
            else:
                sums_all[step, chunk, :, 0] = result
        elif d == 1:
            near_out[step, chunk, 0] = result
            sums_copy(step, chunk, d).start()
        else:
            sums[chunk, sides.index(d), :, 0] = result
            if d:

                @pl.when(jnp.logical_not(inner))
                def _():
                    sums_copy(step, chunk, d).start()

    def mix(step, chunk, side, index):
        if line and step:
            rows, count = sums[chunk, side, index], span_all
        else:
            rows, count = sums_all[step, chunk, index], groups * capacity
        rows = rows.reshape(count, part)
        mixed = jnp.zeros((tok, part), f32)
        for k in range(top_count):
            mixed = mixed + scales[side, k, index] * jnp.dot(
                picks[side, k, index, :, pl.ds(0, count)], rows, preferred_element_type=f32
            )
        return mixed

    def grad_rows(side, index, residual):
        for k in range(top_count):
            values[pl.ds(k * tok, tok)] = (scales[side, k, index] * residual).astype(bf16)
        return jnp.dot(
            picks_t[side, index], values[...], preferred_element_type=f32
        ).astype(bf16).reshape(reach, capacity, part)

    def relay_sums(step, chunk):
        if line:

            @pl.when(inner)
            def _():
                for q in (3, 2):
                    sums_copy(step, chunk, q ^ 1).wait_recv()
                    for index in range(GROUP):
                        dense_out[step, chunk, q - 2, index] = mix(
                            step, chunk, sides.index(q), index
                        ).astype(bf16)
                    dense_copy(step, chunk, q).start()

    def relay_grads(step, chunk):
        if line:

            @pl.when(inner)
            def _():
                for q in (3, 2):
                    even_copy(step, chunk, q).wait_recv()
                    for index in range(GROUP):
                        rows = grad_rows(
                            sides.index(q), index, even_in[step, chunk, q - 2, index].astype(f32)
                        )
                        grad_in[step, chunk, q, index] = rows[0]
                        grad_out[step, chunk, sides.index(q), index] = rows[1]
                    grads_copy(step, chunk, q, 1).start()

    loads[0].wait()
    for position, d in enumerate(order):
        group_copy(d).wait_recv()
        row_copy(d, 2).start()
        row_copy(d, 1).start()
        if position:
            row_copy(chain[position], 2).wait_recv()
            row_copy(chain[position], 3).start()
        compute(chain[position])
        if position == 0:
            lower(1)
            lower(2)
        if position:
            pass_units(chain[position - 1])
        if position == 1:
            for mask in masks:
                state_copy(0, mask).wait_recv()
        if position > 1:
            units_here(chain[position - 1])
            for chunk in range(CHUNKS):
                forward(0, chunk, chain[position - 1])
    row_copy(chain[-1], 2).wait_recv()
    row_copy(chain[-1], 3).start()
    pass_units(chain[-2])
    compute(chain[-1])
    units_here(chain[-2])
    for chunk in range(CHUNKS):
        forward(0, chunk, chain[-2])
    pass_units(chain[-1])
    for which in (1, 2, 3):
        for mask in (2, 3, 1):
            state_copy(which, mask).start()
    units_here(chain[-1])
    for chunk in range(CHUNKS):
        forward(0, chunk, chain[-1])
    units_here(0)
    for chunk in range(CHUNKS):
        forward(0, chunk, 0)
    for which in (1, 2, 3):
        own_slice(which)
    if line:

        @pl.when(inner)
        def _():
            for q in (2, 3):
                far_plan(q).wait_recv()
            for side in (1, 2):
                make_picks(side)

    for mask in masks:
        state_copy(1, mask).wait_recv()

    def residuals(step, chunk):
        if line and step:
            sums_copy(step, chunk, 1).wait_recv()
            dense_copy(step, chunk, 2).wait_recv()
        else:
            for d in order:
                sums_copy(step, chunk, d).wait_recv()
        for index in range(GROUP):
            mixed = mix(step, chunk, 0, index)
            if line and step:
                mixed = mixed + dense_in[step, chunk, index].astype(f32)
            aim = goal[pl.ds(index * tok, tok), columns(chunk)].astype(f32)
            residual = (mixed - aim) * loss_scale
            if line:
                even_out[step, chunk, index] = residual.astype(bf16)
            rows = grad_rows(0, index, residual)
            grad_in[step, chunk, 0, index] = rows[0]
            for d in range(1, reach):
                grad_out[step, chunk, 0 if line else d, index] = rows[d]
        if line:

            @pl.when(inner)
            def _():
                even_copy(step, chunk, 3).start()

            @pl.when(jnp.logical_not(inner))
            def _():
                even_copy(step, chunk, 2).start()

            grads_copy(step, chunk, 0, 1).start()
        else:
            for d in order:
                grads_copy(step, chunk, 0, d).start()

    results = ((moved_rows, moved_out), (first_rows, first_out))

    def out_columns(chunk):
        return pl.ds(pl.multiple_of(member * width + chunk * part, 128), part)

    def out_copy(which, chunk, mask):
        source, target = results[which]
        return push(
            source.at[pl.ds(mask * units, units), columns(chunk)],
            target.at[:, out_columns(chunk)],
            out_send.at[which, chunk, mask - 1], out_recv.at[which, chunk, mask - 1],
            partner(mask),
        )

    def update(step, chunk):
        if line:
            grads_copy(step, chunk, 0, 1).wait_recv()

            @pl.when(jnp.logical_not(inner))
            def _():
                for q in (2, 3):
                    grads_copy(step, chunk, q, 1).wait_recv()
        else:
            for d in order:
                grads_copy(step, chunk, 0, d).wait_recv()
        count = step + 1
        first_fix = 1.0 - 0.9 ** (prior_steps + count)
        second_fix = 1.0 - 0.999 ** (prior_steps + count)
        cols = columns(chunk)
        for mask in (2, 3, 1, 0):
            span = pl.ds(mask * units, units)
            gradient = lax.dot_general(
                hidden[:, :, :, span].reshape(groups * block, units),
                grad_in[step, chunk].reshape(groups * block, part),
                (((0,), (0,)), ((), ())), preferred_element_type=f32,
            )
            one = (first_in if step == 0 else first_two)[span, cols].astype(f32)
            two = (second_in if step == 0 else second_two)[span, cols].astype(f32)
            one = 0.9 * one + 0.1 * gradient
            two = 0.999 * two + 0.001 * gradient * gradient
            change = (one / first_fix) / (jnp.sqrt(two / second_fix) + epsilon)
            if step == 0:
                first_two[span, cols] = one
                second_two[span, cols] = two
                moved_one[span, cols] = change
                old = master_in[span, cols].astype(f32)
                master_two[span, cols] = (old - learn_rate * change).astype(bf16)
            else:
                moved = (moved_one[span, cols] + change).astype(bf16)
                if mask:
                    moved_rows[span, cols] = moved
                    first_rows[span, cols] = one.astype(bf16)
                    for which in range(2):
                        out_copy(which, chunk, mask).start()
                else:
                    moved_out[:, out_columns(chunk)] = moved
                    first_out[:, out_columns(chunk)] = one.astype(bf16)

    def forwards(step, chunk):
        for d in order + [0]:
            forward(step, chunk, d)

    def advance(step, chunk):
        if step == 0 and chunk == 0:
            for which in (2, 3):
                for mask in masks:
                    state_copy(which, mask).wait_recv()
        update(step, chunk)
        if step == 0:
            forwards(1, chunk)

    events = []
    for step in range(2):
        for chunk in range(CHUNKS):
            at = chunk + step * (CHUNKS + 2.5)
            events += [
                (at, residuals, step, chunk), (at + 1.5, relay_grads, step, chunk),
                (at + 2.7, advance, step, chunk),
            ]
            if step == 0:
                events.append((at + 4.3, relay_sums, 1, chunk))
    for _, stage, step, chunk in sorted(events, key=lambda event: event[0]):
        stage(step, chunk)

    for mask in masks:
        plan_copy(mask).wait_send()
        for which in range(4):
            state_copy(which, mask).wait_send()
        for d in chain:
            row_copy(d, mask).wait_send()
            for index in range(GROUP):
                unit_copy(d, mask, index).wait_send()
    for d in order:
        group_copy(d).wait_send()
    for step in range(2):
        for chunk in range(CHUNKS):
            if line:
                grads_copy(step, chunk, 0, 1).wait_send()
                even_copy(step, chunk, 2).wait_send()
            else:
                for d in order:
                    grads_copy(step, chunk, 0, d).wait_send()
            if not (line and step):
                for d in order:
                    sums_copy(step, chunk, d).wait_send()
    for chunk in range(CHUNKS):
        if line:
            sums_copy(1, chunk, 1).wait_send()

            @pl.when(inner)
            def _():
                for q in (2, 3):
                    dense_copy(1, chunk, q).wait_send()
                    for step in range(2):
                        grads_copy(step, chunk, q, 1).wait_send()

            @pl.when(jnp.logical_not(inner))
            def _():
                for q in (2, 3):
                    sums_copy(1, chunk, q).wait_send()

    if line:
        far_plan(2).wait_send()
    for chunk in range(CHUNKS):
        for which in range(2):
            for mask in masks:
                out_copy(which, chunk, mask).wait()


def refit(groups, capacity, home, routes, gates, tokens, targets, gate_up, master, first, second):
    bf16, f32 = jnp.bfloat16, jnp.float32
    top_count, tok = routes.shape
    units, feat = master.shape
    width = feat // GROUP
    vmem = pl.BlockSpec(memory_space=pltpu.VMEM)
    hbm = pl.BlockSpec(memory_space=pl.ANY)
    buffer = lambda *shape, kind=bf16: pltpu.VMEM(shape, kind)
    pair = lambda *shape: [pltpu.SemaphoreType.DMA(shape)] * 2
    part = width // CHUNKS
    line = groups == 4
    sides, reach = (3, 2) if line else (1, groups)
    rows = lambda *shape: buffer(2, CHUNKS, *shape, part)
    return pl.pallas_call(
        functools.partial(refit_kernel, groups, capacity),
        out_shape=[jax.ShapeDtypeStruct((units, feat), bf16)] * 2,
        in_specs=[pl.BlockSpec(memory_space=pltpu.SMEM)] + [vmem] * 4 + [hbm] * 4,
        out_specs=[vmem] * 2,
        scratch_shapes=[
            buffer(groups, capacity, feat),
            buffer(groups, GROUP, capacity, feat),
            buffer(*gate_up.shape),
            buffer(groups, GROUP, capacity, GROUP * units),
            buffer(3, units, feat, kind=f32),
            buffer(3, units, feat),
            *[buffer(GROUP * units, width)] * 3,
            buffer(GROUP * tok, width),
            buffer(sides, GROUP, max(8, 2 * top_count), tok, kind=f32),
            buffer(sides, top_count, GROUP, tok, groups * capacity),
            buffer(sides, GROUP, reach * capacity, top_count * tok),
            buffer(sides, top_count, GROUP, tok, 1, kind=f32),
            rows(GROUP, groups, capacity),
            buffer(CHUNKS, sides, GROUP, 2, capacity, part),
            rows(groups, GROUP, capacity),
            *[rows(2, GROUP, tok) if line else buffer(16, 128)],
            *[rows(GROUP, tok) if line else buffer(16, 128)],
            *[rows(GROUP, tok) if line else buffer(16, 128)],
            *[rows(2, GROUP, tok) if line else buffer(16, 128)],
            rows(sides if line else groups, GROUP, capacity),
            rows(groups, GROUP, capacity),
            buffer(top_count * tok, part),
            buffer(GROUP * units, width),
            *[buffer(GROUP * units, width, kind=f32)] * 3,
            *[buffer(GROUP * units, width)] * 2,
            pltpu.SemaphoreType.DMA((4,)),
            *pair(3), pltpu.SemaphoreType.DMA, pltpu.SemaphoreType.DMA((3,)),
            *pair(groups), *pair(groups, 3), *pair(groups, 3, GROUP), *pair(4, 3),
            *pair(4, CHUNKS, groups), *pair(2, CHUNKS, 3), *pair(2, CHUNKS, 3),
        ],
        compiler_params=pltpu.CompilerParams(
            collective_id=0, has_side_effects=True, vmem_limit_bytes=62 * 2**20
        ),
    )(home, routes, gates, tokens, targets, gate_up, master, first, second)


def shards(tokens, targets, routes, gate_ints, expert_home, gate_up, down_master, moment1, moment2):
    devices = lax.axis_size("expert")
    tok_rows, top_count = routes.shape
    groups = devices // GROUP
    capacity = (5 * tok_rows * top_count * GROUP + 4 * devices - 1) // (4 * devices)
    capacity = -(-capacity // 16) * 16
    moved, moment_one = refit(
        groups, capacity, expert_home, routes.T, gate_ints.T, tokens, targets, gate_up,
        down_master, moment1, moment2,
    )
    return moved.astype(jnp.float32), moment_one.astype(jnp.float32)


def solution(mesh):
    in_specs = (
        P("expert", None),
        P("expert", None),
        P(("cand", "expert"), None),
        P(("cand", "expert"), None),
        P("cand"),
        P(None, ("cand", "expert"), None),
        P(("cand", "expert"), None),
        P(("cand", "expert"), None),
        P(("cand", "expert"), None),
    )
    out_specs = (P(("cand", "expert"), None), P(("cand", "expert"), None))
    return jax.shard_map(shards, mesh=mesh, in_specs=in_specs, out_specs=out_specs, check_vma=False)
```

```python
import functools

import jax
import jax.numpy as jnp
from jax import lax
from jax.experimental import pallas as pl
from jax.experimental.pallas import tpu as pltpu
from jax.sharding import PartitionSpec as P

GROUP = 4
CHUNKS = 4

learn_rate = 0.02
epsilon = 1e-08
prior_steps = 20
loss_scale = 0.125


def xor(index, mask, bits):
    result = index
    for bit in range(bits):
        if mask >> bit & 1:
            result = result + (1 << bit) * (1 - 2 * lax.rem(index // (1 << bit), 2))
    return result


def push(source, target, send_sem, recv_sem, peer):
    return pltpu.make_async_remote_copy(
        src_ref=source,
        dst_ref=target,
        send_sem=send_sem,
        recv_sem=recv_sem,
        device_id={"expert": peer},
        device_id_type=pl.DeviceIdType.MESH,
    )


def refit_kernel(
    groups, capacity,
    home, routes, gates, tokens, targets, gate_up, master, first, second,
    moved_out, first_out,
    outgoing, arrived, weights_in, hidden, loaded, low, master_in, first_in, second_in, goal,
    plan, picks, picks_t, scales, sums_all, sums, near_out, dense_out, dense_in, even_out, even_in,
    grad_out, grad_in, values,
    master_two, first_two, second_two, moved_one, moved_rows, first_rows,
    load_sems, plan_send, plan_recv, far_send, far_recv, group_send, group_recv, row_send, row_recv,
    unit_send, unit_recv, state_send, state_recv, send_sems, recv_sems,
    dense_send, dense_recv, out_send, out_recv,
):
    bf16, f32 = jnp.bfloat16, jnp.float32
    here = lax.axis_index("expert")
    me, member = here // GROUP, lax.rem(here, GROUP)
    base = me * GROUP
    bits = groups.bit_length() - 1
    top_count, tok = routes.shape
    feat = tokens.shape[1]
    units = master.shape[0]
    width = feat // GROUP
    part = width // CHUNKS
    block = GROUP * capacity
    line = groups == 4
    sides = (0, 2, 3) if line else (0,)
    reach = 2 if line else groups
    span_all = reach * capacity
    inner = (me + 1) // 2 == 1
    order = list(range(2, groups)) + [1]
    chain = [0] + order
    masks = range(1, GROUP)

    def group_of(d):
        return xor(me, d, bits)

    def partner(mask):
        return base + xor(member, mask, 2)

    def across(d):
        return group_of(d) * GROUP + member

    loads = [
        pltpu.make_async_copy(source, target, load_sems.at[i])
        for i, (source, target) in enumerate((
            (gate_up, weights_in), (master, loaded.at[0]), (first, loaded.at[1]),
            (second, loaded.at[2]),
        ))
    ]
    for copy in (loads[1], loads[0], loads[2], loads[3]):
        copy.start()

    barrier = pltpu.get_barrier_semaphore()
    peers = [across(d) for d in order] + [partner(mask) for mask in masks]
    for peer in peers:
        pl.semaphore_signal(
            barrier, inc=1, device_id={"expert": peer}, device_id_type=pl.DeviceIdType.MESH
        )

    sub = lax.broadcasted_iota(jnp.int32, (tok, tok), 0)
    lane = lax.broadcasted_iota(jnp.int32, (tok, tok), 1)
    on_diagonal = sub == lane

    def upright(row):
        return jnp.sum(jnp.where(on_diagonal, row, 0.0), axis=1, keepdims=True)

    chosen = [routes[pl.ds(k, 1), :] for k in range(top_count)]
    chosen_f = [c.astype(f32) for c in chosen]
    standing = [upright(c) for c in chosen_f]
    for k in range(top_count):
        same = jnp.zeros((tok, tok), f32)
        for other in range(top_count):
            same = same + jnp.where(standing[other] == chosen_f[k], 1.0, 0.0)
        rank = jnp.sum(jnp.where(sub < lane, same, 0.0), axis=0, keepdims=True)
        place = jnp.zeros((1, tok), jnp.int32)
        for expert in range(home.shape[0]):
            place = place + jnp.where(chosen[k] == expert, home[expert], 0)
        plan[0, 0, pl.ds(k, 1), :] = place.astype(f32) * capacity + rank
        plan[0, 0, pl.ds(top_count + k, 1), :] = gates[pl.ds(k, 1), :].astype(f32) / 4096.0

    def own_rows(d):
        rows = lax.broadcasted_iota(jnp.int32, (capacity, tok), 0) + group_of(d) * capacity
        rows = rows.astype(f32)
        pick = jnp.zeros((capacity, tok), f32)
        for k in range(top_count):
            pick = jnp.where(plan[0, 0, pl.ds(k, 1), :] == rows, 1.0, pick)
        return jnp.dot(pick.astype(bf16), tokens[...], preferred_element_type=f32).astype(bf16)

    def plan_copy(mask):
        return push(
            plan.at[0, 0], plan.at[0, mask], plan_send.at[mask - 1], plan_recv.at[mask - 1],
            partner(mask),
        )

    def group_copy(d):
        return push(
            outgoing.at[d], arrived.at[d, 0], group_send.at[d], group_recv.at[d], across(d)
        )

    def row_copy(d, mask):
        source = arrived.at[d, 2 if mask == 3 else 0]
        return push(
            source, arrived.at[d, mask], row_send.at[d, mask - 1], row_recv.at[d, mask - 1],
            partner(1 if mask == 3 else mask),
        )

    def unit_copy(d, mask, index):
        flip = 1 if mask == 3 else mask
        origin = 2 if mask == 3 else 0
        return push(
            hidden.at[d, index, :, pl.ds(origin * units, units)],
            hidden.at[d, index ^ flip, :, pl.ds(mask * units, units)],
            unit_send.at[d, mask - 1, index], unit_recv.at[d, mask - 1, index], partner(flip),
        )

    states = (
        (low.at[0], master_in), (targets, goal), (low.at[1], first_in), (low.at[2], second_in)
    )

    def state_copy(which, mask):
        source, target = states[which]
        rows = source.shape[0]
        column = pl.multiple_of(xor(member, mask, 2) * width, 128)
        return push(
            source.at[:, pl.ds(column, width)], target.at[pl.ds(mask * rows, rows)],
            state_send.at[which, mask - 1], state_recv.at[which, mask - 1], partner(mask),
        )

    def own_slice(which):
        source, target = states[which]
        column = pl.multiple_of(member * width, 128)
        target[pl.ds(0, source.shape[0])] = source[:, pl.ds(column, width)]

    def far_plan(d):
        return push(plan.at[0], plan.at[d - 1], far_send, far_recv.at[d - 1], across(d))

    def travel(source, target, phase, chunk, d, to):
        return push(
            source, target, send_sems.at[phase, chunk, to], recv_sems.at[phase, chunk, to],
            across(d),
        )

    def sums_copy(step, chunk, d):
        if not (line and step):
            return travel(
                near_out.at[step, chunk, d], sums_all.at[step, chunk, :, d], 2 * step, chunk, d, d
            )
        to = sides.index(d ^ 1)
        source = near_out.at[step, chunk, 0] if d == 1 else sums.at[chunk, d - 1, :, 0]
        return travel(source, sums.at[chunk, to, :, 1], 2 * step, chunk, 1, to)

    def grads_copy(step, chunk, q, d):
        source = grad_out.at[step, chunk, sides.index(q) if line else d]
        to = q ^ 1 if line else d
        return travel(source, grad_in.at[step, chunk, to], 2 * step + 1, chunk, d, to)

    def dense_copy(step, chunk, q):
        return push(
            dense_out.at[step, chunk, q - 2], dense_in.at[step, chunk],
            dense_send.at[step, chunk, q - 2], dense_recv.at[step, chunk, 2], across(q),
        )

    def even_copy(step, chunk, q):
        return push(
            even_out.at[step, chunk], even_in.at[step, chunk, q - 2],
            dense_send.at[step, chunk, 2], dense_recv.at[step, chunk, q - 2], across(q),
        )

    def columns(chunk):
        return pl.ds(chunk * part, part)

    def lower(which):
        loads[which + 1].wait()

        @pl.loop(0, units // 16)
        def _(tile):
            span = pl.ds(pl.multiple_of(tile * 16, 16), 16)
            low[which, span] = loaded[which, span].astype(bf16)

    pl.semaphore_wait(barrier, len(peers))
    early = order[: groups // 4]
    arrived[0, 0] = own_rows(0)
    row_copy(0, 2).start()
    row_copy(0, 1).start()
    for d in order:
        outgoing[d] = own_rows(d)
        if d in early:
            group_copy(d).start()
    for mask in masks:
        plan_copy(mask).start()
    lower(0)
    row_copy(0, 2).wait_recv()
    row_copy(0, 3).start()
    for d in order:
        if d not in early:
            group_copy(d).start()
    for mask in (2, 3, 1):
        state_copy(0, mask).start()
    own_slice(0)
    for mask in masks:
        plan_copy(mask).wait_recv()

    def make_picks(side):
        @pl.loop(0, GROUP)
        def _(index):
            for k in range(top_count):
                scales[side, k, index] = upright(plan[side, index, pl.ds(top_count + k, 1), :])
                slot = upright(plan[side, index, pl.ds(k, 1), :])
                for d in range(reach if side else groups):
                    rows = lax.broadcasted_iota(jnp.int32, (tok, capacity), 1)
                    rows = (rows + group_of(d) * capacity).astype(f32)
                    picks[side, k, index, :, pl.ds(d * capacity, capacity)] = jnp.where(
                        slot == rows, 1.0, 0.0
                    ).astype(bf16)
            for d in range(reach):
                rows = lax.broadcasted_iota(jnp.int32, (capacity, tok), 0)
                rows = (rows + group_of(d) * capacity).astype(f32)
                for k in range(top_count):
                    picks_t[
                        side, index, pl.ds(d * capacity, capacity), pl.ds(k * tok, tok)
                    ] = jnp.where(
                        plan[side, index, pl.ds(k, 1), :] == rows, 1.0, 0.0
                    ).astype(bf16)

    if line:

        @pl.when(inner)
        def _():
            far_plan(3).start()

        @pl.when(jnp.logical_not(inner))
        def _():
            far_plan(2).start()

    make_picks(0)

    def compute(d):
        row_copy(d, 1).wait_recv()
        row_copy(d, 3).wait_recv()
        acts = [
            lax.dot_general(
                arrived[d].reshape(block, feat), weights_in[i], (((1,), (1,)), ((), ())),
                preferred_element_type=f32,
            )
            for i in range(2)
        ]
        gated = acts[0] / (1.0 + jnp.exp(-acts[0])) * acts[1]
        hidden[d, :, :, pl.ds(0, units)] = gated.astype(bf16).reshape(GROUP, capacity, units)

    def send_units(d):
        for mask in (2, 1):
            for index in range(GROUP):
                unit_copy(d, mask, index).start()

    def pass_units(d):
        for index in range(GROUP):
            unit_copy(d, 2, index).wait_recv()
        for index in range(GROUP):
            unit_copy(d, 3, index).start()

    def units_here(d):
        for index in range(GROUP):
            unit_copy(d, 1, index).wait_recv()
            unit_copy(d, 3, index).wait_recv()

    def forward(step, chunk, d):
        weight = master_in if step == 0 else master_two
        result = jnp.dot(
            hidden[d].reshape(block, GROUP * units), weight[:, columns(chunk)],
            preferred_element_type=f32,
        ).astype(bf16).reshape(GROUP, capacity, part)
        if not (line and step):
            if d:
                near_out[step, chunk, d] = result
                sums_copy(step, chunk, d).start()
            else:
                sums_all[step, chunk, :, 0] = result
        elif d == 1:
            near_out[step, chunk, 0] = result
            sums_copy(step, chunk, d).start()
        else:
            sums[chunk, sides.index(d), :, 0] = result
            if d:

                @pl.when(jnp.logical_not(inner))
                def _():
                    sums_copy(step, chunk, d).start()

    def mix(step, chunk, side, index):
        if line and step:
            rows, count = sums[chunk, side, index], span_all
        else:
            rows, count = sums_all[step, chunk, index], groups * capacity
        rows = rows.reshape(count, part)
        mixed = jnp.zeros((tok, part), f32)
        for k in range(top_count):
            mixed = mixed + scales[side, k, index] * jnp.dot(
                picks[side, k, index, :, pl.ds(0, count)], rows, preferred_element_type=f32
            )
        return mixed

    def grad_rows(side, index, residual):
        for k in range(top_count):
            values[pl.ds(k * tok, tok)] = (scales[side, k, index] * residual).astype(bf16)
        return jnp.dot(
            picks_t[side, index], values[...], preferred_element_type=f32
        ).astype(bf16).reshape(reach, capacity, part)

    def relay_sums(step, chunk):
        if line:

            @pl.when(inner)
            def _():
                for q in (3, 2):
                    sums_copy(step, chunk, q ^ 1).wait_recv()

                    @pl.loop(0, GROUP, unroll=2)
                    def _(index):
                        dense_out[step, chunk, q - 2, index] = mix(
                            step, chunk, sides.index(q), index
                        ).astype(bf16)

                    dense_copy(step, chunk, q).start()

    def relay_grads(step, chunk):
        if line:

            @pl.when(inner)
            def _():
                for q in (3, 2):
                    even_copy(step, chunk, q).wait_recv()

                    @pl.loop(0, GROUP, unroll=2)
                    def _(index):
                        rows = grad_rows(
                            sides.index(q), index, even_in[step, chunk, q - 2, index].astype(f32)
                        )
                        grad_in[step, chunk, q, index] = rows[0]
                        grad_out[step, chunk, sides.index(q), index] = rows[1]

                    grads_copy(step, chunk, q, 1).start()

    loads[0].wait()
    for position, d in enumerate(order):
        group_copy(d).wait_recv()
        row_copy(d, 2).start()
        row_copy(d, 1).start()
        if position == 0:
            compute(0)
            lower(1)
            lower(2)
            continue
        before = order[position - 1]
        row_copy(before, 2).wait_recv()
        row_copy(before, 3).start()
        compute(before)
        send_units(before)
        if position == 1:
            for mask in masks:
                state_copy(0, mask).wait_recv()
        else:
            pass_units(order[position - 2])
            units_here(order[position - 2])
            for chunk in range(CHUNKS):
                forward(0, chunk, order[position - 2])
    row_copy(order[-1], 2).wait_recv()
    row_copy(order[-1], 3).start()
    pass_units(order[-2])
    compute(order[-1])
    send_units(order[-1])
    send_units(0)
    units_here(order[-2])
    for chunk in range(CHUNKS):
        forward(0, chunk, order[-2])
    pass_units(order[-1])
    for which in (1, 2, 3):
        for mask in (2, 3, 1):
            state_copy(which, mask).start()
    units_here(order[-1])
    for chunk in range(CHUNKS):
        forward(0, chunk, order[-1])
    pass_units(0)
    units_here(0)
    for chunk in range(CHUNKS):
        forward(0, chunk, 0)
    for which in (1, 2, 3):
        own_slice(which)
    if line:

        @pl.when(inner)
        def _():
            for q in (2, 3):
                far_plan(q).wait_recv()
            for side in (1, 2):
                make_picks(side)

    for mask in masks:
        state_copy(1, mask).wait_recv()

    def residuals(step, chunk):
        if line and step:
            sums_copy(step, chunk, 1).wait_recv()
            dense_copy(step, chunk, 2).wait_recv()
        else:
            for d in order:
                sums_copy(step, chunk, d).wait_recv()

        @pl.loop(0, GROUP, unroll=2)
        def _(index):
            mixed = mix(step, chunk, 0, index)
            if line and step:
                mixed = mixed + dense_in[step, chunk, index].astype(f32)
            aim = goal[pl.ds(pl.multiple_of(index * tok, tok), tok), columns(chunk)].astype(f32)
            residual = (mixed - aim) * loss_scale
            if line:
                even_out[step, chunk, index] = residual.astype(bf16)
            rows = grad_rows(0, index, residual)
            grad_in[step, chunk, 0, index] = rows[0]
            for d in range(1, reach):
                grad_out[step, chunk, 0 if line else d, index] = rows[d]

        if line:

            @pl.when(inner)
            def _():
                even_copy(step, chunk, 3).start()

            @pl.when(jnp.logical_not(inner))
            def _():
                even_copy(step, chunk, 2).start()

            grads_copy(step, chunk, 0, 1).start()
        else:
            for d in order:
                grads_copy(step, chunk, 0, d).start()

    results = ((moved_rows, moved_out), (first_rows, first_out))

    def out_columns(chunk):
        return pl.ds(pl.multiple_of(member * width + chunk * part, 128), part)

    def out_copy(which, chunk, mask):
        source, target = results[which]
        return push(
            source.at[pl.ds(mask * units, units), columns(chunk)],
            target.at[:, out_columns(chunk)],
            out_send.at[which, chunk, mask - 1], out_recv.at[which, chunk, mask - 1],
            partner(mask),
        )

    def update(step, chunk):
        if line:
            grads_copy(step, chunk, 0, 1).wait_recv()

            @pl.when(jnp.logical_not(inner))
            def _():
                for q in (2, 3):
                    grads_copy(step, chunk, q, 1).wait_recv()
        else:
            for d in order:
                grads_copy(step, chunk, 0, d).wait_recv()
        count = step + 1
        first_fix = 1.0 - 0.9 ** (prior_steps + count)
        second_fix = 1.0 - 0.999 ** (prior_steps + count)
        cols = columns(chunk)

        def tile_of(mask):
            span = pl.ds(pl.multiple_of(mask * units, units), units)
            gradient = lax.dot_general(
                hidden[:, :, :, span].reshape(groups * block, units),
                grad_in[step, chunk].reshape(groups * block, part),
                (((0,), (0,)), ((), ())), preferred_element_type=f32,
            )
            one = (first_in if step == 0 else first_two)[span, cols].astype(f32)
            two = (second_in if step == 0 else second_two)[span, cols].astype(f32)
            one = 0.9 * one + 0.1 * gradient
            two = 0.999 * two + 0.001 * gradient * gradient
            change = (one / first_fix) / (jnp.sqrt(two / second_fix) + epsilon)
            if step == 0:
                first_two[span, cols] = one
                second_two[span, cols] = two
                moved_one[span, cols] = change
                old = master_in[span, cols].astype(f32)
                master_two[span, cols] = (old - learn_rate * change).astype(bf16)
            else:
                moved_rows[span, cols] = (moved_one[span, cols] + change).astype(bf16)
                first_rows[span, cols] = one.astype(bf16)

        if step == 0:

            @pl.loop(0, GROUP)
            def _(mask):
                tile_of(mask)
        else:

            @pl.loop(0, GROUP)
            def _(turn):
                mask = lax.rem(turn + 2, GROUP)
                tile_of(mask)
                for mask in masks:

                    @pl.when(turn == (mask + 2) % GROUP)
                    def _():
                        for which in range(2):
                            out_copy(which, chunk, mask).start()

            for source, target in results:
                target[:, out_columns(chunk)] = source[pl.ds(0, units), cols]

    def forwards(step, chunk):
        for d in order + [0]:
            forward(step, chunk, d)

    def advance(step, chunk):
        if step == 0 and chunk == 0:
            for which in (2, 3):
                for mask in masks:
                    state_copy(which, mask).wait_recv()
        update(step, chunk)
        if step == 0:
            forwards(1, chunk)

    events = []
    for step in range(2):
        for chunk in range(CHUNKS):
            at = chunk + step * (CHUNKS + 2.5)
            events += [
                (at, residuals, step, chunk), (at + 1.5, relay_grads, step, chunk),
                (at + 2.7, advance, step, chunk),
            ]
            if step == 0:
                events.append((at + 4.3, relay_sums, 1, chunk))
    for _, stage, step, chunk in sorted(events, key=lambda event: event[0]):
        stage(step, chunk)

    for mask in masks:
        plan_copy(mask).wait_send()
        for which in range(4):
            state_copy(which, mask).wait_send()
        for d in chain:
            row_copy(d, mask).wait_send()
            for index in range(GROUP):
                unit_copy(d, mask, index).wait_send()
    for d in order:
        group_copy(d).wait_send()
    for step in range(2):
        for chunk in range(CHUNKS):
            if line:
                grads_copy(step, chunk, 0, 1).wait_send()
                even_copy(step, chunk, 2).wait_send()
            else:
                for d in order:
                    grads_copy(step, chunk, 0, d).wait_send()
            if not (line and step):
                for d in order:
                    sums_copy(step, chunk, d).wait_send()
    for chunk in range(CHUNKS):
        if line:
            sums_copy(1, chunk, 1).wait_send()

            @pl.when(inner)
            def _():
                for q in (2, 3):
                    dense_copy(1, chunk, q).wait_send()
                    for step in range(2):
                        grads_copy(step, chunk, q, 1).wait_send()

            @pl.when(jnp.logical_not(inner))
            def _():
                for q in (2, 3):
                    sums_copy(1, chunk, q).wait_send()

    if line:
        far_plan(2).wait_send()
    for chunk in range(CHUNKS):
        for which in range(2):
            for mask in masks:
                out_copy(which, chunk, mask).wait()


def refit(groups, capacity, home, routes, gates, tokens, targets, gate_up, master, first, second):
    bf16, f32 = jnp.bfloat16, jnp.float32
    top_count, tok = routes.shape
    units, feat = master.shape
    width = feat // GROUP
    vmem = pl.BlockSpec(memory_space=pltpu.VMEM)
    hbm = pl.BlockSpec(memory_space=pl.ANY)
    buffer = lambda *shape, kind=bf16: pltpu.VMEM(shape, kind)
    pair = lambda *shape: [pltpu.SemaphoreType.DMA(shape)] * 2
    part = width // CHUNKS
    line = groups == 4
    sides, reach = (3, 2) if line else (1, groups)
    rows = lambda *shape: buffer(2, CHUNKS, *shape, part)
    return pl.pallas_call(
        functools.partial(refit_kernel, groups, capacity),
        out_shape=[jax.ShapeDtypeStruct((units, feat), bf16)] * 2,
        in_specs=[pl.BlockSpec(memory_space=pltpu.SMEM)] + [vmem] * 4 + [hbm] * 4,
        out_specs=[vmem] * 2,
        scratch_shapes=[
            buffer(groups, capacity, feat),
            buffer(groups, GROUP, capacity, feat),
            buffer(*gate_up.shape),
            buffer(groups, GROUP, capacity, GROUP * units),
            buffer(3, units, feat, kind=f32),
            buffer(3, units, feat),
            *[buffer(GROUP * units, width)] * 3,
            buffer(GROUP * tok, width),
            buffer(sides, GROUP, max(8, 2 * top_count), tok, kind=f32),
            buffer(sides, top_count, GROUP, tok, groups * capacity),
            buffer(sides, GROUP, reach * capacity, top_count * tok),
            buffer(sides, top_count, GROUP, tok, 1, kind=f32),
            rows(GROUP, groups, capacity),
            buffer(CHUNKS, sides, GROUP, 2, capacity, part),
            rows(groups, GROUP, capacity),
            *[rows(2, GROUP, tok) if line else buffer(16, 128)],
            *[rows(GROUP, tok) if line else buffer(16, 128)],
            *[rows(GROUP, tok) if line else buffer(16, 128)],
            *[rows(2, GROUP, tok) if line else buffer(16, 128)],
            rows(sides if line else groups, GROUP, capacity),
            rows(groups, GROUP, capacity),
            buffer(top_count * tok, part),
            buffer(GROUP * units, width),
            *[buffer(GROUP * units, width, kind=f32)] * 3,
            *[buffer(GROUP * units, width)] * 2,
            pltpu.SemaphoreType.DMA((4,)),
            *pair(3), pltpu.SemaphoreType.DMA, pltpu.SemaphoreType.DMA((3,)),
            *pair(groups), *pair(groups, 3), *pair(groups, 3, GROUP), *pair(4, 3),
            *pair(4, CHUNKS, groups), *pair(2, CHUNKS, 3), *pair(2, CHUNKS, 3),
        ],
        compiler_params=pltpu.CompilerParams(
            collective_id=0, has_side_effects=True, vmem_limit_bytes=62 * 2**20
        ),
    )(home, routes, gates, tokens, targets, gate_up, master, first, second)


def shards(tokens, targets, routes, gate_ints, expert_home, gate_up, down_master, moment1, moment2):
    devices = lax.axis_size("expert")
    tok_rows, top_count = routes.shape
    groups = devices // GROUP
    capacity = (5 * tok_rows * top_count * GROUP + 4 * devices - 1) // (4 * devices)
    capacity = -(-capacity // 16) * 16
    moved, moment_one = refit(
        groups, capacity, expert_home, routes.T, gate_ints.T, tokens, targets, gate_up,
        down_master, moment1, moment2,
    )
    return moved.astype(jnp.float32), moment_one.astype(jnp.float32)


def solution(mesh):
    in_specs = (
        P("expert", None),
        P("expert", None),
        P(("cand", "expert"), None),
        P(("cand", "expert"), None),
        P("cand"),
        P(None, ("cand", "expert"), None),
        P(("cand", "expert"), None),
        P(("cand", "expert"), None),
        P(("cand", "expert"), None),
    )
    out_specs = (P(("cand", "expert"), None), P(("cand", "expert"), None))
    return jax.shard_map(shards, mesh=mesh, in_specs=in_specs, out_specs=out_specs, check_vma=False)
```

```python
import functools

import jax
import jax.numpy as jnp
from jax import lax
from jax.experimental import pallas as pl
from jax.experimental.pallas import tpu as pltpu
from jax.sharding import PartitionSpec as P

GROUP = 4
CHUNKS = 4

learn_rate = 0.02
epsilon = 1e-08
prior_steps = 20
loss_scale = 0.125


def xor(index, mask, bits):
    result = index
    for bit in range(bits):
        if mask >> bit & 1:
            result = result + (1 << bit) * (1 - 2 * lax.rem(index // (1 << bit), 2))
    return result


def push(source, target, send_sem, recv_sem, peer):
    return pltpu.make_async_remote_copy(
        src_ref=source,
        dst_ref=target,
        send_sem=send_sem,
        recv_sem=recv_sem,
        device_id={"expert": peer},
        device_id_type=pl.DeviceIdType.MESH,
    )


def refit_kernel(
    groups, capacity,
    home, routes, gates, tokens, targets, gate_up, master, first, second,
    moved_out, first_out,
    outgoing, arrived, weights_in, hidden, hidden_t, loaded, low, master_in, first_in, second_in, goal,
    plan, picks, picks_t, scales, sums_all, sums, near_out, dense_out, dense_in, even_out, even_in,
    grad_out, grad_in, values,
    master_two, first_two, second_two, moved_one, moved_rows, first_rows,
    load_sems, plan_send, plan_recv, far_send, far_recv, group_send, group_recv, row_send, row_recv,
    unit_send, unit_recv, state_send, state_recv, send_sems, recv_sems,
    dense_send, dense_recv, out_send, out_recv,
):
    bf16, f32 = jnp.bfloat16, jnp.float32
    here = lax.axis_index("expert")
    me, member = here // GROUP, lax.rem(here, GROUP)
    base = me * GROUP
    bits = groups.bit_length() - 1
    top_count, tok = routes.shape
    feat = tokens.shape[1]
    units = master.shape[0]
    width = feat // GROUP
    part = width // CHUNKS
    block = GROUP * capacity
    line = groups == 4
    sides = (0, 2, 3) if line else (0,)
    reach = 2 if line else groups
    span_all = reach * capacity
    inner = (me + 1) // 2 == 1
    order = list(range(2, groups)) + [1]
    chain = [0] + order
    masks = range(1, GROUP)

    def group_of(d):
        return xor(me, d, bits)

    def partner(mask):
        return base + xor(member, mask, 2)

    def across(d):
        return group_of(d) * GROUP + member

    loads = [
        pltpu.make_async_copy(source, target, load_sems.at[i])
        for i, (source, target) in enumerate((
            (gate_up, weights_in), (master, loaded.at[0]), (first, loaded.at[1]),
            (second, loaded.at[2]),
        ))
    ]
    for copy in (loads[1], loads[0], loads[2], loads[3]):
        copy.start()

    barrier = pltpu.get_barrier_semaphore()
    peers = [across(d) for d in order] + [partner(mask) for mask in masks]
    for peer in peers:
        pl.semaphore_signal(
            barrier, inc=1, device_id={"expert": peer}, device_id_type=pl.DeviceIdType.MESH
        )

    sub = lax.broadcasted_iota(jnp.int32, (tok, tok), 0)
    lane = lax.broadcasted_iota(jnp.int32, (tok, tok), 1)
    on_diagonal = sub == lane

    def upright(row):
        return jnp.sum(jnp.where(on_diagonal, row, 0.0), axis=1, keepdims=True)

    chosen = [routes[pl.ds(k, 1), :] for k in range(top_count)]
    chosen_f = [c.astype(f32) for c in chosen]
    standing = [upright(c) for c in chosen_f]
    for k in range(top_count):
        same = jnp.zeros((tok, tok), f32)
        for other in range(top_count):
            same = same + jnp.where(standing[other] == chosen_f[k], 1.0, 0.0)
        rank = jnp.sum(jnp.where(sub < lane, same, 0.0), axis=0, keepdims=True)
        place = jnp.zeros((1, tok), jnp.int32)
        for expert in range(home.shape[0]):
            place = place + jnp.where(chosen[k] == expert, home[expert], 0)
        plan[0, 0, pl.ds(k, 1), :] = place.astype(f32) * capacity + rank
        plan[0, 0, pl.ds(top_count + k, 1), :] = gates[pl.ds(k, 1), :].astype(f32) / 4096.0

    def own_rows(d):
        rows = lax.broadcasted_iota(jnp.int32, (capacity, tok), 0) + group_of(d) * capacity
        rows = rows.astype(f32)
        pick = jnp.zeros((capacity, tok), f32)
        for k in range(top_count):
            pick = jnp.where(plan[0, 0, pl.ds(k, 1), :] == rows, 1.0, pick)
        return jnp.dot(pick.astype(bf16), tokens[...], preferred_element_type=f32).astype(bf16)

    def plan_copy(mask):
        return push(
            plan.at[0, 0], plan.at[0, mask], plan_send.at[mask - 1], plan_recv.at[mask - 1],
            partner(mask),
        )

    def group_copy(d):
        return push(
            outgoing.at[d], arrived.at[d, 0], group_send.at[d], group_recv.at[d], across(d)
        )

    def row_copy(d, mask):
        source = arrived.at[d, 2 if mask == 3 else 0]
        return push(
            source, arrived.at[d, mask], row_send.at[d, mask - 1], row_recv.at[d, mask - 1],
            partner(1 if mask == 3 else mask),
        )

    def unit_copy(d, mask, index):
        flip = 1 if mask == 3 else mask
        origin = 2 if mask == 3 else 0
        return push(
            hidden.at[d, index, :, pl.ds(origin * units, units)],
            hidden.at[d, index ^ flip, :, pl.ds(mask * units, units)],
            unit_send.at[d, mask - 1, index], unit_recv.at[d, mask - 1, index], partner(flip),
        )

    states = (
        (low.at[0], master_in), (targets, goal), (low.at[1], first_in), (low.at[2], second_in)
    )

    def state_copy(which, mask):
        source, target = states[which]
        rows = source.shape[0]
        column = pl.multiple_of(xor(member, mask, 2) * width, 128)
        return push(
            source.at[:, pl.ds(column, width)], target.at[pl.ds(mask * rows, rows)],
            state_send.at[which, mask - 1], state_recv.at[which, mask - 1], partner(mask),
        )

    def own_slice(which):
        source, target = states[which]
        column = pl.multiple_of(member * width, 128)
        target[pl.ds(0, source.shape[0])] = source[:, pl.ds(column, width)]

    def far_plan(d):
        return push(plan.at[0], plan.at[d - 1], far_send, far_recv.at[d - 1], across(d))

    def travel(source, target, phase, chunk, d, to):
        return push(
            source, target, send_sems.at[phase, chunk, to], recv_sems.at[phase, chunk, to],
            across(d),
        )

    def sums_copy(step, chunk, d):
        if not (line and step):
            return travel(
                near_out.at[step, chunk, d], sums_all.at[step, chunk, :, d], 2 * step, chunk, d, d
            )
        to = sides.index(d ^ 1)
        source = near_out.at[step, chunk, 0] if d == 1 else sums.at[chunk, d - 1, :, 0]
        return travel(source, sums.at[chunk, to, :, 1], 2 * step, chunk, 1, to)

    def grads_copy(step, chunk, q, d):
        source = grad_out.at[step, chunk, sides.index(q) if line else d]
        to = q ^ 1 if line else d
        return travel(source, grad_in.at[step, chunk, to], 2 * step + 1, chunk, d, to)

    def dense_copy(step, chunk, q):
        return push(
            dense_out.at[step, chunk, q - 2], dense_in.at[step, chunk],
            dense_send.at[step, chunk, q - 2], dense_recv.at[step, chunk, 2], across(q),
        )

    def even_copy(step, chunk, q):
        return push(
            even_out.at[step, chunk], even_in.at[step, chunk, q - 2],
            dense_send.at[step, chunk, 2], dense_recv.at[step, chunk, q - 2], across(q),
        )

    def columns(chunk):
        return pl.ds(chunk * part, part)

    def lower(which):
        loads[which + 1].wait()

        @pl.loop(0, units // 16)
        def _(tile):
            span = pl.ds(pl.multiple_of(tile * 16, 16), 16)
            low[which, span] = loaded[which, span].astype(bf16)

    pl.semaphore_wait(barrier, len(peers))
    early = order[: groups // 4]
    arrived[0, 0] = own_rows(0)
    row_copy(0, 2).start()
    row_copy(0, 1).start()
    for d in order:
        outgoing[d] = own_rows(d)
        if d in early:
            group_copy(d).start()
    for mask in masks:
        plan_copy(mask).start()
    lower(0)
    row_copy(0, 2).wait_recv()
    row_copy(0, 3).start()
    for d in order:
        if d not in early:
            group_copy(d).start()
    for mask in (2, 3, 1):
        state_copy(0, mask).start()
    own_slice(0)
    for mask in masks:
        plan_copy(mask).wait_recv()

    def make_picks(side):
        @pl.loop(0, GROUP)
        def _(index):
            for k in range(top_count):
                scales[side, k, index] = upright(plan[side, index, pl.ds(top_count + k, 1), :])
                slot = upright(plan[side, index, pl.ds(k, 1), :])
                for d in range(reach if side else groups):
                    rows = lax.broadcasted_iota(jnp.int32, (tok, capacity), 1)
                    rows = (rows + group_of(d) * capacity).astype(f32)
                    picks[side, k, index, :, pl.ds(d * capacity, capacity)] = jnp.where(
                        slot == rows, 1.0, 0.0
                    ).astype(bf16)
            for d in range(reach):
                rows = lax.broadcasted_iota(jnp.int32, (capacity, tok), 0)
                rows = (rows + group_of(d) * capacity).astype(f32)
                for k in range(top_count):
                    picks_t[
                        side, index, pl.ds(d * capacity, capacity), pl.ds(k * tok, tok)
                    ] = jnp.where(
                        plan[side, index, pl.ds(k, 1), :] == rows, 1.0, 0.0
                    ).astype(bf16)

    if line:

        @pl.when(inner)
        def _():
            far_plan(3).start()

        @pl.when(jnp.logical_not(inner))
        def _():
            far_plan(2).start()

    make_picks(0)

    def compute(d):
        row_copy(d, 1).wait_recv()
        row_copy(d, 3).wait_recv()
        acts = [
            lax.dot_general(
                arrived[d].reshape(block, feat), weights_in[i], (((1,), (1,)), ((), ())),
                preferred_element_type=f32,
            )
            for i in range(2)
        ]
        gated = acts[0] / (1.0 + jnp.exp(-acts[0])) * acts[1]
        hidden[d, :, :, pl.ds(0, units)] = gated.astype(bf16).reshape(GROUP, capacity, units)

    def send_units(d):
        for mask in (2, 1):
            for index in range(GROUP):
                unit_copy(d, mask, index).start()

    def pass_units(d):
        for index in range(GROUP):
            unit_copy(d, 2, index).wait_recv()
        for index in range(GROUP):
            unit_copy(d, 3, index).start()

    def units_here(d):
        for index in range(GROUP):
            unit_copy(d, 1, index).wait_recv()
            unit_copy(d, 3, index).wait_recv()

    def forward(step, chunk, d):
        weight = master_in if step == 0 else master_two
        result = jnp.dot(
            hidden[d].reshape(block, GROUP * units), weight[:, columns(chunk)],
            preferred_element_type=f32,
        ).astype(bf16).reshape(GROUP, capacity, part)
        if not (line and step):
            if d:
                near_out[step, chunk, d] = result
                sums_copy(step, chunk, d).start()
            else:
                sums_all[step, chunk, :, 0] = result
        elif d == 1:
            near_out[step, chunk, 0] = result
            sums_copy(step, chunk, d).start()
        else:
            sums[chunk, sides.index(d), :, 0] = result
            if d:

                @pl.when(jnp.logical_not(inner))
                def _():
                    sums_copy(step, chunk, d).start()

    def mix(step, chunk, side, index):
        if line and step:
            rows, count = sums[chunk, side, index], span_all
        else:
            rows, count = sums_all[step, chunk, index], groups * capacity
        rows = rows.reshape(count, part)
        mixed = jnp.zeros((tok, part), f32)
        for k in range(top_count):
            mixed = mixed + scales[side, k, index] * jnp.dot(
                picks[side, k, index, :, pl.ds(0, count)], rows, preferred_element_type=f32
            )
        return mixed

    def grad_rows(side, index, residual):
        for k in range(top_count):
            values[pl.ds(k * tok, tok)] = (scales[side, k, index] * residual).astype(bf16)
        return jnp.dot(
            picks_t[side, index], values[...], preferred_element_type=f32
        ).astype(bf16).reshape(reach, capacity, part)

    def relay_sums(step, chunk):
        if line:

            @pl.when(inner)
            def _():
                for q in (3, 2):
                    sums_copy(step, chunk, q ^ 1).wait_recv()

                    @pl.loop(0, GROUP, unroll=2)
                    def _(index):
                        dense_out[step, chunk, q - 2, index] = mix(
                            step, chunk, sides.index(q), index
                        ).astype(bf16)

                    dense_copy(step, chunk, q).start()

    def relay_grads(step, chunk):
        if line:

            @pl.when(inner)
            def _():
                for q in (3, 2):
                    even_copy(step, chunk, q).wait_recv()

                    @pl.loop(0, GROUP, unroll=2)
                    def _(index):
                        rows = grad_rows(
                            sides.index(q), index, even_in[step, chunk, q - 2, index].astype(f32)
                        )
                        grad_in[step, chunk, q, index] = rows[0]
                        grad_out[step, chunk, sides.index(q), index] = rows[1]

                    grads_copy(step, chunk, q, 1).start()

    loads[0].wait()
    for position, d in enumerate(order):
        group_copy(d).wait_recv()
        row_copy(d, 2).start()
        row_copy(d, 1).start()
        if position == 0:
            compute(0)
            lower(1)
            lower(2)
            continue
        before = order[position - 1]
        row_copy(before, 2).wait_recv()
        row_copy(before, 3).start()
        compute(before)
        send_units(before)
        if position == 1:
            for mask in masks:
                state_copy(0, mask).wait_recv()
        else:
            pass_units(order[position - 2])
            units_here(order[position - 2])
            for chunk in range(CHUNKS):
                forward(0, chunk, order[position - 2])
    row_copy(order[-1], 2).wait_recv()
    row_copy(order[-1], 3).start()
    pass_units(order[-2])
    compute(order[-1])
    send_units(order[-1])
    send_units(0)
    units_here(order[-2])
    for chunk in range(CHUNKS):
        forward(0, chunk, order[-2])
    pass_units(order[-1])
    for which in (1, 2, 3):
        for mask in (2, 3, 1):
            state_copy(which, mask).start()
    units_here(order[-1])
    for chunk in range(CHUNKS):
        forward(0, chunk, order[-1])
    pass_units(0)
    units_here(0)
    for chunk in range(CHUNKS):
        forward(0, chunk, 0)
    for which in (1, 2, 3):
        own_slice(which)

    if line:

        @pl.loop(0, GROUP)
        def _(mask):
            span = pl.ds(pl.multiple_of(mask * units, units), units)
            hidden_t[span] = hidden[:, :, :, span].reshape(groups * block, units).T

    if line:

        @pl.when(inner)
        def _():
            for q in (2, 3):
                far_plan(q).wait_recv()
            for side in (1, 2):
                make_picks(side)

    for mask in masks:
        state_copy(1, mask).wait_recv()

    def residuals(step, chunk):
        if line and step:
            sums_copy(step, chunk, 1).wait_recv()
            dense_copy(step, chunk, 2).wait_recv()
        else:
            for d in order:
                sums_copy(step, chunk, d).wait_recv()

        @pl.loop(0, GROUP, unroll=2)
        def _(index):
            mixed = mix(step, chunk, 0, index)
            if line and step:
                mixed = mixed + dense_in[step, chunk, index].astype(f32)
            aim = goal[pl.ds(pl.multiple_of(index * tok, tok), tok), columns(chunk)].astype(f32)
            residual = (mixed - aim) * loss_scale
            if line:
                even_out[step, chunk, index] = residual.astype(bf16)
            rows = grad_rows(0, index, residual)
            grad_in[step, chunk, 0, index] = rows[0]
            for d in range(1, reach):
                grad_out[step, chunk, 0 if line else d, index] = rows[d]

        if line:

            @pl.when(inner)
            def _():
                even_copy(step, chunk, 3).start()

            @pl.when(jnp.logical_not(inner))
            def _():
                even_copy(step, chunk, 2).start()

            grads_copy(step, chunk, 0, 1).start()
        else:
            for d in order:
                grads_copy(step, chunk, 0, d).start()

    results = ((moved_rows, moved_out), (first_rows, first_out))

    def out_columns(chunk):
        return pl.ds(pl.multiple_of(member * width + chunk * part, 128), part)

    def out_copy(which, chunk, mask):
        source, target = results[which]
        return push(
            source.at[pl.ds(mask * units, units), columns(chunk)],
            target.at[:, out_columns(chunk)],
            out_send.at[which, chunk, mask - 1], out_recv.at[which, chunk, mask - 1],
            partner(mask),
        )

    def update(step, chunk):
        if line:
            grads_copy(step, chunk, 0, 1).wait_recv()

            @pl.when(jnp.logical_not(inner))
            def _():
                for q in (2, 3):
                    grads_copy(step, chunk, q, 1).wait_recv()
        else:
            for d in order:
                grads_copy(step, chunk, 0, d).wait_recv()
        count = step + 1
        first_fix = 1.0 - 0.9 ** (prior_steps + count)
        second_fix = 1.0 - 0.999 ** (prior_steps + count)
        cols = columns(chunk)

        def tile_of(mask):
            span = pl.ds(pl.multiple_of(mask * units, units), units)
            arrivals = grad_in[step, chunk].reshape(groups * block, part)
            if line:
                gradient = jnp.dot(hidden_t[span], arrivals, preferred_element_type=f32)
            else:
                gradient = lax.dot_general(
                    hidden[:, :, :, span].reshape(groups * block, units), arrivals,
                    (((0,), (0,)), ((), ())), preferred_element_type=f32,
                )
            one = (first_in if step == 0 else first_two)[span, cols].astype(f32)
            two = (second_in if step == 0 else second_two)[span, cols].astype(f32)
            one = 0.9 * one + 0.1 * gradient
            two = 0.999 * two + 0.001 * gradient * gradient
            change = (one / first_fix) / (jnp.sqrt(two / second_fix) + epsilon)
            if step == 0:
                first_two[span, cols] = one
                second_two[span, cols] = two
                moved_one[span, cols] = change
                old = master_in[span, cols].astype(f32)
                master_two[span, cols] = (old - learn_rate * change).astype(bf16)
            else:
                moved_rows[span, cols] = (moved_one[span, cols] + change).astype(bf16)
                first_rows[span, cols] = one.astype(bf16)

        if step == 0:

            @pl.loop(0, GROUP)
            def _(mask):
                tile_of(mask)
        else:

            @pl.loop(0, GROUP)
            def _(turn):
                mask = lax.rem(turn + 2, GROUP)
                tile_of(mask)
                for mask in masks:

                    @pl.when(turn == (mask + 2) % GROUP)
                    def _():
                        for which in range(2):
                            out_copy(which, chunk, mask).start()

            for source, target in results:
                target[:, out_columns(chunk)] = source[pl.ds(0, units), cols]

    def forwards(step, chunk):
        for d in order + [0]:
            forward(step, chunk, d)

    def advance(step, chunk):
        if step == 0 and chunk == 0:
            for which in (2, 3):
                for mask in masks:
                    state_copy(which, mask).wait_recv()
        update(step, chunk)
        if step == 0:
            forwards(1, chunk)

    events = []
    for step in range(2):
        for chunk in range(CHUNKS):
            at = chunk + step * (CHUNKS + 2.5)
            events += [
                (at, residuals, step, chunk), (at + 1.5, relay_grads, step, chunk),
                (at + 2.7, advance, step, chunk),
            ]
            if step == 0:
                events.append((at + 4.3, relay_sums, 1, chunk))
    for _, stage, step, chunk in sorted(events, key=lambda event: event[0]):
        stage(step, chunk)

    for mask in masks:
        plan_copy(mask).wait_send()
        for which in range(4):
            state_copy(which, mask).wait_send()
        for d in chain:
            row_copy(d, mask).wait_send()
            for index in range(GROUP):
                unit_copy(d, mask, index).wait_send()
    for d in order:
        group_copy(d).wait_send()
    for step in range(2):
        for chunk in range(CHUNKS):
            if line:
                grads_copy(step, chunk, 0, 1).wait_send()
                even_copy(step, chunk, 2).wait_send()
            else:
                for d in order:
                    grads_copy(step, chunk, 0, d).wait_send()
            if not (line and step):
                for d in order:
                    sums_copy(step, chunk, d).wait_send()
    for chunk in range(CHUNKS):
        if line:
            sums_copy(1, chunk, 1).wait_send()

            @pl.when(inner)
            def _():
                for q in (2, 3):
                    dense_copy(1, chunk, q).wait_send()
                    for step in range(2):
                        grads_copy(step, chunk, q, 1).wait_send()

            @pl.when(jnp.logical_not(inner))
            def _():
                for q in (2, 3):
                    sums_copy(1, chunk, q).wait_send()

    if line:
        far_plan(2).wait_send()
    for chunk in range(CHUNKS):
        for which in range(2):
            for mask in masks:
                out_copy(which, chunk, mask).wait()


def refit(groups, capacity, home, routes, gates, tokens, targets, gate_up, master, first, second):
    bf16, f32 = jnp.bfloat16, jnp.float32
    top_count, tok = routes.shape
    units, feat = master.shape
    width = feat // GROUP
    vmem = pl.BlockSpec(memory_space=pltpu.VMEM)
    hbm = pl.BlockSpec(memory_space=pl.ANY)
    buffer = lambda *shape, kind=bf16: pltpu.VMEM(shape, kind)
    pair = lambda *shape: [pltpu.SemaphoreType.DMA(shape)] * 2
    part = width // CHUNKS
    line = groups == 4
    sides, reach = (3, 2) if line else (1, groups)
    rows = lambda *shape: buffer(2, CHUNKS, *shape, part)
    return pl.pallas_call(
        functools.partial(refit_kernel, groups, capacity),
        out_shape=[jax.ShapeDtypeStruct((units, feat), bf16)] * 2,
        in_specs=[pl.BlockSpec(memory_space=pltpu.SMEM)] + [vmem] * 4 + [hbm] * 4,
        out_specs=[vmem] * 2,
        scratch_shapes=[
            buffer(groups, capacity, feat),
            buffer(groups, GROUP, capacity, feat),
            buffer(*gate_up.shape),
            buffer(groups, GROUP, capacity, GROUP * units),
            buffer(GROUP * units, groups * GROUP * capacity) if line else buffer(16, 128),
            buffer(3, units, feat, kind=f32),
            buffer(3, units, feat),
            *[buffer(GROUP * units, width)] * 3,
            buffer(GROUP * tok, width),
            buffer(sides, GROUP, max(8, 2 * top_count), tok, kind=f32),
            buffer(sides, top_count, GROUP, tok, groups * capacity),
            buffer(sides, GROUP, reach * capacity, top_count * tok),
            buffer(sides, top_count, GROUP, tok, 1, kind=f32),
            rows(GROUP, groups, capacity),
            buffer(CHUNKS, sides, GROUP, 2, capacity, part),
            rows(groups, GROUP, capacity),
            *[rows(2, GROUP, tok) if line else buffer(16, 128)],
            *[rows(GROUP, tok) if line else buffer(16, 128)],
            *[rows(GROUP, tok) if line else buffer(16, 128)],
            *[rows(2, GROUP, tok) if line else buffer(16, 128)],
            rows(sides if line else groups, GROUP, capacity),
            rows(groups, GROUP, capacity),
            buffer(top_count * tok, part),
            buffer(GROUP * units, width),
            *[buffer(GROUP * units, width, kind=f32)] * 3,
            *[buffer(GROUP * units, width)] * 2,
            pltpu.SemaphoreType.DMA((4,)),
            *pair(3), pltpu.SemaphoreType.DMA, pltpu.SemaphoreType.DMA((3,)),
            *pair(groups), *pair(groups, 3), *pair(groups, 3, GROUP), *pair(4, 3),
            *pair(4, CHUNKS, groups), *pair(2, CHUNKS, 3), *pair(2, CHUNKS, 3),
        ],
        compiler_params=pltpu.CompilerParams(
            collective_id=0, has_side_effects=True, vmem_limit_bytes=62 * 2**20
        ),
    )(home, routes, gates, tokens, targets, gate_up, master, first, second)


def shards(tokens, targets, routes, gate_ints, expert_home, gate_up, down_master, moment1, moment2):
    devices = lax.axis_size("expert")
    tok_rows, top_count = routes.shape
    groups = devices // GROUP
    capacity = (5 * tok_rows * top_count * GROUP + 4 * devices - 1) // (4 * devices)
    capacity = -(-capacity // 16) * 16
    moved, moment_one = refit(
        groups, capacity, expert_home, routes.T, gate_ints.T, tokens, targets, gate_up,
        down_master, moment1, moment2,
    )
    return moved.astype(jnp.float32), moment_one.astype(jnp.float32)


def solution(mesh):
    in_specs = (
        P("expert", None),
        P("expert", None),
        P(("cand", "expert"), None),
        P(("cand", "expert"), None),
        P("cand"),
        P(None, ("cand", "expert"), None),
        P(("cand", "expert"), None),
        P(("cand", "expert"), None),
        P(("cand", "expert"), None),
    )
    out_specs = (P(("cand", "expert"), None), P(("cand", "expert"), None))
    return jax.shard_map(shards, mesh=mesh, in_specs=in_specs, out_specs=out_specs, check_vma=False)
```

```python
import functools

import jax
import jax.numpy as jnp
from jax import lax
from jax.experimental import pallas as pl
from jax.experimental.pallas import tpu as pltpu
from jax.sharding import PartitionSpec as P

GROUP = 4
CHUNKS = 4

learn_rate = 0.02
epsilon = 1e-08
prior_steps = 20
loss_scale = 0.125


def xor(index, mask, bits):
    result = index
    for bit in range(bits):
        if mask >> bit & 1:
            result = result + (1 << bit) * (1 - 2 * lax.rem(index // (1 << bit), 2))
    return result


def push(source, target, send_sem, recv_sem, peer):
    return pltpu.make_async_remote_copy(
        src_ref=source,
        dst_ref=target,
        send_sem=send_sem,
        recv_sem=recv_sem,
        device_id={"expert": peer},
        device_id_type=pl.DeviceIdType.MESH,
    )


def refit_kernel(
    groups, capacity,
    home, routes, gates, tokens, targets, gate_up, master, first, second,
    moved_out, first_out,
    outgoing, arrived, weights_in, hidden, hidden_t, loaded, low, master_in, first_in, second_in, goal,
    plan, picks, picks_t, scales, sums_all, sums, near_out, dense_out, dense_in, even_out, even_in,
    grad_out, grad_in, values,
    master_two, first_two, second_two, moved_one, moved_rows, first_rows,
    load_sems, plan_send, plan_recv, far_send, far_recv, group_send, group_recv, row_send, row_recv,
    unit_send, unit_recv, state_send, state_recv, send_sems, recv_sems,
    dense_send, dense_recv, out_send, out_recv,
):
    bf16, f32 = jnp.bfloat16, jnp.float32
    here = lax.axis_index("expert")
    me, member = here // GROUP, lax.rem(here, GROUP)
    base = me * GROUP
    bits = groups.bit_length() - 1
    top_count, tok = routes.shape
    feat = tokens.shape[1]
    units = master.shape[0]
    width = feat // GROUP
    part = width // CHUNKS
    block = GROUP * capacity
    line = groups == 4
    sides = (0, 2, 3) if line else (0,)
    reach = 2 if line else groups
    span_all = reach * capacity
    inner = (me + 1) // 2 == 1
    order = list(range(2, groups)) + [1]
    chain = [0] + order
    masks = range(1, GROUP)

    def group_of(d):
        return xor(me, d, bits)

    def partner(mask):
        return base + xor(member, mask, 2)

    def across(d):
        return group_of(d) * GROUP + member

    loads = [
        pltpu.make_async_copy(source, target, load_sems.at[i])
        for i, (source, target) in enumerate((
            (gate_up, weights_in), (master, loaded.at[0]), (first, loaded.at[1]),
            (second, loaded.at[2]),
        ))
    ]
    for copy in (loads[1], loads[0], loads[2], loads[3]):
        copy.start()

    barrier = pltpu.get_barrier_semaphore()
    peers = [across(d) for d in order] + [partner(mask) for mask in masks]
    for peer in peers:
        pl.semaphore_signal(
            barrier, inc=1, device_id={"expert": peer}, device_id_type=pl.DeviceIdType.MESH
        )

    sub = lax.broadcasted_iota(jnp.int32, (tok, tok), 0)
    lane = lax.broadcasted_iota(jnp.int32, (tok, tok), 1)
    on_diagonal = sub == lane

    def upright(row):
        return jnp.sum(jnp.where(on_diagonal, row, 0.0), axis=1, keepdims=True)

    chosen = [routes[pl.ds(k, 1), :] for k in range(top_count)]
    chosen_f = [c.astype(f32) for c in chosen]
    standing = [upright(c) for c in chosen_f]
    for k in range(top_count):
        same = jnp.zeros((tok, tok), f32)
        for other in range(top_count):
            same = same + jnp.where(standing[other] == chosen_f[k], 1.0, 0.0)
        rank = jnp.sum(jnp.where(sub < lane, same, 0.0), axis=0, keepdims=True)
        place = jnp.zeros((1, tok), jnp.int32)
        for expert in range(home.shape[0]):
            place = place + jnp.where(chosen[k] == expert, home[expert], 0)
        plan[0, 0, pl.ds(k, 1), :] = place.astype(f32) * capacity + rank
        plan[0, 0, pl.ds(top_count + k, 1), :] = gates[pl.ds(k, 1), :].astype(f32) / 4096.0

    def own_rows(d):
        rows = lax.broadcasted_iota(jnp.int32, (capacity, tok), 0) + group_of(d) * capacity
        rows = rows.astype(f32)
        pick = jnp.zeros((capacity, tok), f32)
        for k in range(top_count):
            pick = jnp.where(plan[0, 0, pl.ds(k, 1), :] == rows, 1.0, pick)
        return jnp.dot(pick.astype(bf16), tokens[...], preferred_element_type=f32).astype(bf16)

    def plan_copy(mask):
        return push(
            plan.at[0, 0], plan.at[0, mask], plan_send.at[mask - 1], plan_recv.at[mask - 1],
            partner(mask),
        )

    def group_copy(d):
        return push(
            outgoing.at[d], arrived.at[d, 0], group_send.at[d], group_recv.at[d], across(d)
        )

    def row_copy(d, mask):
        source = arrived.at[d, 2 if mask == 3 else 0]
        return push(
            source, arrived.at[d, mask], row_send.at[d, mask - 1], row_recv.at[d, mask - 1],
            partner(1 if mask == 3 else mask),
        )

    def unit_copy(d, mask, index):
        flip = 1 if mask == 3 else mask
        origin = 2 if mask == 3 else 0
        return push(
            hidden.at[d, index, :, pl.ds(origin * units, units)],
            hidden.at[d, index ^ flip, :, pl.ds(mask * units, units)],
            unit_send.at[d, mask - 1, index], unit_recv.at[d, mask - 1, index], partner(flip),
        )

    states = (
        (low.at[0], master_in), (targets, goal), (low.at[1], first_in), (low.at[2], second_in)
    )

    def state_copy(which, mask):
        source, target = states[which]
        rows = source.shape[0]
        column = pl.multiple_of(xor(member, mask, 2) * width, 128)
        return push(
            source.at[:, pl.ds(column, width)], target.at[pl.ds(mask * rows, rows)],
            state_send.at[which, mask - 1], state_recv.at[which, mask - 1], partner(mask),
        )

    def own_slice(which):
        source, target = states[which]
        column = pl.multiple_of(member * width, 128)
        target[pl.ds(0, source.shape[0])] = source[:, pl.ds(column, width)]

    def far_plan(d):
        return push(plan.at[0], plan.at[d - 1], far_send, far_recv.at[d - 1], across(d))

    def travel(source, target, phase, chunk, d, to):
        return push(
            source, target, send_sems.at[phase, chunk, to], recv_sems.at[phase, chunk, to],
            across(d),
        )

    def sums_copy(step, chunk, d):
        if not (line and step):
            return travel(
                near_out.at[step, chunk, d], sums_all.at[step, chunk, :, d], 2 * step, chunk, d, d
            )
        to = sides.index(d ^ 1)
        source = near_out.at[step, chunk, 0] if d == 1 else sums.at[chunk, d - 1, :, 0]
        return travel(source, sums.at[chunk, to, :, 1], 2 * step, chunk, 1, to)

    def grads_copy(step, chunk, q, d):
        source = grad_out.at[step, chunk, sides.index(q) if line else d]
        to = q ^ 1 if line else d
        return travel(source, grad_in.at[step, chunk, to], 2 * step + 1, chunk, d, to)

    def dense_copy(step, chunk, q):
        return push(
            dense_out.at[step, chunk, q - 2], dense_in.at[step, chunk],
            dense_send.at[step, chunk, q - 2], dense_recv.at[step, chunk, 2], across(q),
        )

    def even_copy(step, chunk, q):
        return push(
            even_out.at[step, chunk], even_in.at[step, chunk, q - 2],
            dense_send.at[step, chunk, 2], dense_recv.at[step, chunk, q - 2], across(q),
        )

    def columns(chunk):
        return pl.ds(chunk * part, part)

    def lower(which):
        loads[which + 1].wait()

        @pl.loop(0, units // 16)
        def _(tile):
            span = pl.ds(pl.multiple_of(tile * 16, 16), 16)
            low[which, span] = loaded[which, span].astype(bf16)

    pl.semaphore_wait(barrier, len(peers))
    early = order[: groups // 4]
    arrived[0, 0] = own_rows(0)
    row_copy(0, 2).start()
    row_copy(0, 1).start()
    for d in order:
        outgoing[d] = own_rows(d)
        if d in early:
            group_copy(d).start()
    for mask in masks:
        plan_copy(mask).start()
    lower(0)
    row_copy(0, 2).wait_recv()
    row_copy(0, 3).start()
    for d in order:
        if d not in early:
            group_copy(d).start()
    for mask in (2, 3, 1):
        state_copy(0, mask).start()
    own_slice(0)
    for mask in masks:
        plan_copy(mask).wait_recv()

    def make_picks(side):
        @pl.loop(0, GROUP)
        def _(index):
            for k in range(top_count):
                scales[side, k, index] = upright(plan[side, index, pl.ds(top_count + k, 1), :])
                slot = upright(plan[side, index, pl.ds(k, 1), :])
                for d in range(reach if side else groups):
                    rows = lax.broadcasted_iota(jnp.int32, (tok, capacity), 1)
                    rows = (rows + group_of(d) * capacity).astype(f32)
                    picks[side, k, index, :, pl.ds(d * capacity, capacity)] = jnp.where(
                        slot == rows, 1.0, 0.0
                    ).astype(bf16)
            for d in range(reach):
                rows = lax.broadcasted_iota(jnp.int32, (capacity, tok), 0)
                rows = (rows + group_of(d) * capacity).astype(f32)
                for k in range(top_count):
                    picks_t[
                        side, index, pl.ds(d * capacity, capacity), pl.ds(k * tok, tok)
                    ] = jnp.where(
                        plan[side, index, pl.ds(k, 1), :] == rows, 1.0, 0.0
                    ).astype(bf16)

    if line:

        @pl.when(inner)
        def _():
            far_plan(3).start()

        @pl.when(jnp.logical_not(inner))
        def _():
            far_plan(2).start()

    make_picks(0)

    def compute(d):
        row_copy(d, 1).wait_recv()
        row_copy(d, 3).wait_recv()
        acts = [
            lax.dot_general(
                arrived[d].reshape(block, feat), weights_in[i], (((1,), (1,)), ((), ())),
                preferred_element_type=f32,
            )
            for i in range(2)
        ]
        gated = acts[0] / (1.0 + jnp.exp(-acts[0])) * acts[1]
        hidden[d, :, :, pl.ds(0, units)] = gated.astype(bf16).reshape(GROUP, capacity, units)

    def send_units(d):
        for mask in (2, 1):
            for index in range(GROUP):
                unit_copy(d, mask, index).start()

    def pass_units(d):
        for index in range(GROUP):
            unit_copy(d, 2, index).wait_recv()
        for index in range(GROUP):
            unit_copy(d, 3, index).start()

    def units_here(d):
        for index in range(GROUP):
            unit_copy(d, 1, index).wait_recv()
            unit_copy(d, 3, index).wait_recv()

    def forward_pair(chunk, d):
        both = jnp.dot(
            hidden[d].reshape(block, GROUP * units), master_in[:, pl.ds(chunk * part, 2 * part)],
            preferred_element_type=f32,
        ).astype(bf16)
        for half in range(2):
            result = both[:, half * part:(half + 1) * part].reshape(GROUP, capacity, part)
            hand_over(0, chunk + half, d, result)

    def first_forward(d):
        for chunk in range(0, CHUNKS, 2):
            forward_pair(chunk, d)

    def forward(step, chunk, d):
        result = jnp.dot(
            hidden[d].reshape(block, GROUP * units), master_two[:, columns(chunk)],
            preferred_element_type=f32,
        ).astype(bf16).reshape(GROUP, capacity, part)
        hand_over(step, chunk, d, result)

    def hand_over(step, chunk, d, result):
        if not (line and step):
            if d:
                near_out[step, chunk, d] = result
                sums_copy(step, chunk, d).start()
            else:
                sums_all[step, chunk, :, 0] = result
        elif d == 1:
            near_out[step, chunk, 0] = result
            sums_copy(step, chunk, d).start()
        else:
            sums[chunk, sides.index(d), :, 0] = result
            if d:

                @pl.when(jnp.logical_not(inner))
                def _():
                    sums_copy(step, chunk, d).start()

    def mix(step, chunk, side, index):
        if line and step:
            rows, count = sums[chunk, side, index], span_all
        else:
            rows, count = sums_all[step, chunk, index], groups * capacity
        rows = rows.reshape(count, part)
        mixed = jnp.zeros((tok, part), f32)
        for k in range(top_count):
            mixed = mixed + scales[side, k, index] * jnp.dot(
                picks[side, k, index, :, pl.ds(0, count)], rows, preferred_element_type=f32
            )
        return mixed

    def grad_rows(side, index, residual):
        for k in range(top_count):
            values[pl.ds(k * tok, tok)] = (scales[side, k, index] * residual).astype(bf16)
        return jnp.dot(
            picks_t[side, index], values[...], preferred_element_type=f32
        ).astype(bf16).reshape(reach, capacity, part)

    def relay_sums(step, chunk):
        if line:

            @pl.when(inner)
            def _():
                for q in (3, 2):
                    sums_copy(step, chunk, q ^ 1).wait_recv()

                    @pl.loop(0, GROUP, unroll=2)
                    def _(index):
                        dense_out[step, chunk, q - 2, index] = mix(
                            step, chunk, sides.index(q), index
                        ).astype(bf16)

                    dense_copy(step, chunk, q).start()

    def relay_grads(step, chunk):
        if line:

            @pl.when(inner)
            def _():
                for q in (3, 2):
                    even_copy(step, chunk, q).wait_recv()

                    @pl.loop(0, GROUP, unroll=2)
                    def _(index):
                        rows = grad_rows(
                            sides.index(q), index, even_in[step, chunk, q - 2, index].astype(f32)
                        )
                        grad_in[step, chunk, q, index] = rows[0]
                        grad_out[step, chunk, sides.index(q), index] = rows[1]

                    grads_copy(step, chunk, q, 1).start()

    loads[0].wait()
    for position, d in enumerate(order):
        group_copy(d).wait_recv()
        row_copy(d, 2).start()
        row_copy(d, 1).start()
        if position == 0:
            compute(0)
            lower(1)
            lower(2)
            continue
        before = order[position - 1]
        row_copy(before, 2).wait_recv()
        row_copy(before, 3).start()
        compute(before)
        send_units(before)
        if position == 1:
            for mask in masks:
                state_copy(0, mask).wait_recv()
        else:
            pass_units(order[position - 2])
            units_here(order[position - 2])
            first_forward(order[position - 2])
    row_copy(order[-1], 2).wait_recv()
    row_copy(order[-1], 3).start()
    pass_units(order[-2])
    compute(order[-1])
    send_units(order[-1])
    send_units(0)
    units_here(order[-2])
    first_forward(order[-2])
    pass_units(order[-1])
    for which in (1, 2, 3):
        for mask in (2, 3, 1):
            state_copy(which, mask).start()
    units_here(order[-1])
    first_forward(order[-1])
    pass_units(0)
    units_here(0)
    first_forward(0)
    for which in (1, 2, 3):
        own_slice(which)

    if line:

        @pl.loop(0, GROUP)
        def _(mask):
            span = pl.ds(pl.multiple_of(mask * units, units), units)
            hidden_t[span] = hidden[:, :, :, span].reshape(groups * block, units).T

    if line:

        @pl.when(inner)
        def _():
            for q in (2, 3):
                far_plan(q).wait_recv()
            for side in (1, 2):
                make_picks(side)

    for mask in masks:
        state_copy(1, mask).wait_recv()

    def residuals(step, chunk):
        if line and step:
            sums_copy(step, chunk, 1).wait_recv()
            dense_copy(step, chunk, 2).wait_recv()
        else:
            for d in order:
                sums_copy(step, chunk, d).wait_recv()

        @pl.loop(0, GROUP, unroll=2)
        def _(index):
            mixed = mix(step, chunk, 0, index)
            if line and step:
                mixed = mixed + dense_in[step, chunk, index].astype(f32)
            aim = goal[pl.ds(pl.multiple_of(index * tok, tok), tok), columns(chunk)].astype(f32)
            residual = (mixed - aim) * loss_scale
            if line:
                even_out[step, chunk, index] = residual.astype(bf16)
            rows = grad_rows(0, index, residual)
            grad_in[step, chunk, 0, index] = rows[0]
            for d in range(1, reach):
                grad_out[step, chunk, 0 if line else d, index] = rows[d]

        if line:

            @pl.when(inner)
            def _():
                even_copy(step, chunk, 3).start()

            @pl.when(jnp.logical_not(inner))
            def _():
                even_copy(step, chunk, 2).start()

            grads_copy(step, chunk, 0, 1).start()
        else:
            for d in order:
                grads_copy(step, chunk, 0, d).start()

    results = ((moved_rows, moved_out), (first_rows, first_out))

    def out_columns(chunk):
        return pl.ds(pl.multiple_of(member * width + chunk * part, 128), part)

    def out_copy(which, chunk, mask):
        source, target = results[which]
        return push(
            source.at[pl.ds(mask * units, units), columns(chunk)],
            target.at[:, out_columns(chunk)],
            out_send.at[which, chunk, mask - 1], out_recv.at[which, chunk, mask - 1],
            partner(mask),
        )

    def update(step, chunk):
        if line:
            grads_copy(step, chunk, 0, 1).wait_recv()

            @pl.when(jnp.logical_not(inner))
            def _():
                for q in (2, 3):
                    grads_copy(step, chunk, q, 1).wait_recv()
        else:
            for d in order:
                grads_copy(step, chunk, 0, d).wait_recv()
        count = step + 1
        first_fix = 1.0 - 0.9 ** (prior_steps + count)
        second_fix = 1.0 - 0.999 ** (prior_steps + count)
        cols = columns(chunk)

        def tile_of(mask):
            span = pl.ds(pl.multiple_of(mask * units, units), units)
            arrivals = grad_in[step, chunk].reshape(groups * block, part)
            if line:
                gradient = jnp.dot(hidden_t[span], arrivals, preferred_element_type=f32)
            else:
                gradient = lax.dot_general(
                    hidden[:, :, :, span].reshape(groups * block, units), arrivals,
                    (((0,), (0,)), ((), ())), preferred_element_type=f32,
                )
            one = (first_in if step == 0 else first_two)[span, cols].astype(f32)
            two = (second_in if step == 0 else second_two)[span, cols].astype(f32)
            one = 0.9 * one + 0.1 * gradient
            two = 0.999 * two + 0.001 * gradient * gradient
            change = (one / first_fix) / (jnp.sqrt(two / second_fix) + epsilon)
            if step == 0:
                first_two[span, cols] = one
                second_two[span, cols] = two
                moved_one[span, cols] = change
                old = master_in[span, cols].astype(f32)
                master_two[span, cols] = (old - learn_rate * change).astype(bf16)
            else:
                moved_rows[span, cols] = (moved_one[span, cols] + change).astype(bf16)
                first_rows[span, cols] = one.astype(bf16)

        if step == 0:

            @pl.loop(0, GROUP)
            def _(mask):
                tile_of(mask)
        else:

            @pl.loop(0, GROUP)
            def _(turn):
                mask = lax.rem(turn + 2, GROUP)
                tile_of(mask)
                for mask in masks:

                    @pl.when(turn == (mask + 2) % GROUP)
                    def _():
                        for which in range(2):
                            out_copy(which, chunk, mask).start()

            for source, target in results:
                target[:, out_columns(chunk)] = source[pl.ds(0, units), cols]

    def forwards(step, chunk):
        for d in order + [0]:
            forward(step, chunk, d)

    def advance(step, chunk):
        if step == 0 and chunk == 0:
            for which in (2, 3):
                for mask in masks:
                    state_copy(which, mask).wait_recv()
        update(step, chunk)
        if step == 0:
            forwards(1, chunk)

    events = []
    for step in range(2):
        for chunk in range(CHUNKS):
            at = chunk + step * (CHUNKS + 2.5)
            events += [
                (at, residuals, step, chunk), (at + 1.5, relay_grads, step, chunk),
                (at + 2.7, advance, step, chunk),
            ]
            if step == 0:
                events.append((at + 4.3, relay_sums, 1, chunk))
    for _, stage, step, chunk in sorted(events, key=lambda event: event[0]):
        stage(step, chunk)

    for mask in masks:
        plan_copy(mask).wait_send()
        for which in range(4):
            state_copy(which, mask).wait_send()
        for d in chain:
            row_copy(d, mask).wait_send()
            for index in range(GROUP):
                unit_copy(d, mask, index).wait_send()
    for d in order:
        group_copy(d).wait_send()
    for step in range(2):
        for chunk in range(CHUNKS):
            if line:
                grads_copy(step, chunk, 0, 1).wait_send()
                even_copy(step, chunk, 2).wait_send()
            else:
                for d in order:
                    grads_copy(step, chunk, 0, d).wait_send()
            if not (line and step):
                for d in order:
                    sums_copy(step, chunk, d).wait_send()
    for chunk in range(CHUNKS):
        if line:
            sums_copy(1, chunk, 1).wait_send()

            @pl.when(inner)
            def _():
                for q in (2, 3):
                    dense_copy(1, chunk, q).wait_send()
                    for step in range(2):
                        grads_copy(step, chunk, q, 1).wait_send()

            @pl.when(jnp.logical_not(inner))
            def _():
                for q in (2, 3):
                    sums_copy(1, chunk, q).wait_send()

    if line:
        far_plan(2).wait_send()
    for chunk in range(CHUNKS):
        for which in range(2):
            for mask in masks:
                out_copy(which, chunk, mask).wait()


def refit(groups, capacity, home, routes, gates, tokens, targets, gate_up, master, first, second):
    bf16, f32 = jnp.bfloat16, jnp.float32
    top_count, tok = routes.shape
    units, feat = master.shape
    width = feat // GROUP
    vmem = pl.BlockSpec(memory_space=pltpu.VMEM)
    hbm = pl.BlockSpec(memory_space=pl.ANY)
    buffer = lambda *shape, kind=bf16: pltpu.VMEM(shape, kind)
    pair = lambda *shape: [pltpu.SemaphoreType.DMA(shape)] * 2
    part = width // CHUNKS
    line = groups == 4
    sides, reach = (3, 2) if line else (1, groups)
    rows = lambda *shape: buffer(2, CHUNKS, *shape, part)
    return pl.pallas_call(
        functools.partial(refit_kernel, groups, capacity),
        out_shape=[jax.ShapeDtypeStruct((units, feat), bf16)] * 2,
        in_specs=[pl.BlockSpec(memory_space=pltpu.SMEM)] + [vmem] * 4 + [hbm] * 4,
        out_specs=[vmem] * 2,
        scratch_shapes=[
            buffer(groups, capacity, feat),
            buffer(groups, GROUP, capacity, feat),
            buffer(*gate_up.shape),
            buffer(groups, GROUP, capacity, GROUP * units),
            buffer(GROUP * units, groups * GROUP * capacity) if line else buffer(16, 128),
            buffer(3, units, feat, kind=f32),
            buffer(3, units, feat),
            *[buffer(GROUP * units, width)] * 3,
            buffer(GROUP * tok, width),
            buffer(sides, GROUP, max(8, 2 * top_count), tok, kind=f32),
            buffer(sides, top_count, GROUP, tok, groups * capacity),
            buffer(sides, GROUP, reach * capacity, top_count * tok),
            buffer(sides, top_count, GROUP, tok, 1, kind=f32),
            rows(GROUP, groups, capacity),
            buffer(CHUNKS, sides, GROUP, 2, capacity, part),
            rows(groups, GROUP, capacity),
            *[rows(2, GROUP, tok) if line else buffer(16, 128)],
            *[rows(GROUP, tok) if line else buffer(16, 128)],
            *[rows(GROUP, tok) if line else buffer(16, 128)],
            *[rows(2, GROUP, tok) if line else buffer(16, 128)],
            rows(sides if line else groups, GROUP, capacity),
            rows(groups, GROUP, capacity),
            buffer(top_count * tok, part),
            buffer(GROUP * units, width),
            *[buffer(GROUP * units, width, kind=f32)] * 3,
            *[buffer(GROUP * units, width)] * 2,
            pltpu.SemaphoreType.DMA((4,)),
            *pair(3), pltpu.SemaphoreType.DMA, pltpu.SemaphoreType.DMA((3,)),
            *pair(groups), *pair(groups, 3), *pair(groups, 3, GROUP), *pair(4, 3),
            *pair(4, CHUNKS, groups), *pair(2, CHUNKS, 3), *pair(2, CHUNKS, 3),
        ],
        compiler_params=pltpu.CompilerParams(
            collective_id=0, has_side_effects=True, vmem_limit_bytes=62 * 2**20
        ),
    )(home, routes, gates, tokens, targets, gate_up, master, first, second)


def shards(tokens, targets, routes, gate_ints, expert_home, gate_up, down_master, moment1, moment2):
    devices = lax.axis_size("expert")
    tok_rows, top_count = routes.shape
    groups = devices // GROUP
    capacity = (5 * tok_rows * top_count * GROUP + 4 * devices - 1) // (4 * devices)
    capacity = -(-capacity // 16) * 16
    moved, moment_one = refit(
        groups, capacity, expert_home, routes.T, gate_ints.T, tokens, targets, gate_up,
        down_master, moment1, moment2,
    )
    return moved.astype(jnp.float32), moment_one.astype(jnp.float32)


def solution(mesh):
    in_specs = (
        P("expert", None),
        P("expert", None),
        P(("cand", "expert"), None),
        P(("cand", "expert"), None),
        P("cand"),
        P(None, ("cand", "expert"), None),
        P(("cand", "expert"), None),
        P(("cand", "expert"), None),
        P(("cand", "expert"), None),
    )
    out_specs = (P(("cand", "expert"), None), P(("cand", "expert"), None))
    return jax.shard_map(shards, mesh=mesh, in_specs=in_specs, out_specs=out_specs, check_vma=False)
```
